1024 devices in a mesh: slab: 16 (over y, z_hi), chan: 64 (over x, z_lo, core).
Axes of the slice: x: 4, y: 4, z: 32 (z_hi: 4, z_lo: 8; z = z_hi * 8 + z_lo), core: 2. Of those that a mesh axis runs over, the one named last changes fastest.
Arguments:
- x_in: bfloat16 [256, 32, 8, 128], P('chan', 'slab'), may hold values from -6 to 6
- weight: bfloat16 [256, 27, 256], P('chan'), may hold values from -0.21875 to 0.21875
- bias_vec: bfloat16 [256], P('chan'), may hold values from -3 to 3
- grad_out: bfloat16 [256, 32, 8, 128], P('chan', 'slab'), may hold values from -6 to 6
Outputs:
- activation: bfloat16 [256, 32, 8, 128], P('chan', 'slab')
- input_grad: bfloat16 [256, 32, 8, 128], P('chan', 'slab')
- weight_grad: float32 [256, 27, 256], P('chan')
- bias_grad: float32 [256], P('chan')
The draws below stay inside these ranges and needn't reach their ends.
All inputs are finite; a program needn't handle non-finite values.
Results may differ from the reference program's by a relative error of at most 0.008.
Values may be sent and summed in bfloat16 or wider, within the bound.
A program may use at most 32 MiB of HBM per device.

```python
import math
import jax
import jax.numpy as jnp
from jax import lax

CIN = 256
COUT = 256
NY = 8
NZ = 128
NX = 32


def spiked(values, stream_key, source, target, parts, factor):
    owner, partner = [(jnp.arange(values.shape[position]) // (values.shape[position] // parts)).reshape([-1 if axis == position else 1 for axis in range(values.ndim)]) for position in (source, target)]
    chosen = jax.random.permutation(stream_key, parts)[partner]
    strong = (owner == chosen) | (owner == (partner + parts // 2) % parts)
    return jnp.where(strong, factor * values, values)


def steps_of(key, shape, split, least, top_value):
    def one(dim, shards_of):
        draws = jax.random.uniform(jax.random.fold_in(jax.random.fold_in(key, 6), dim), (shards_of,), jnp.float32, least / len(split), top_value / len(split))
        return jnp.repeat(jnp.exp(draws), shape[dim] // shards_of).reshape((-1,) + (1,) * (len(shape) - dim - 1))

    level = one(*split[0])
    for cut in split[1:]:
        level = level * one(*cut)
    return level


def bell_draw(own_key, shape, width, limit, pieces=(), held_as=jnp.bfloat16):
    array = width * jax.random.normal(own_key, shape, jnp.float32)
    if pieces:
        array = array * steps_of(own_key, shape, pieces, -0.22, 0.18)
    return jnp.clip(array, -limit, limit).astype(held_as)


def noise_with(own_key, extent, deviation, bound, pieces, heavy, kind=jnp.bfloat16):
    result = deviation * jax.random.normal(own_key, extent, jnp.float32)
    if pieces:
        result = result * steps_of(own_key, extent, pieces, -0.22, 0.18)
    return jnp.clip(spiked(result, jax.random.fold_in(own_key, 3), *heavy), -bound, bound).astype(kind)


def setup_inputs(seed: int = 0) -> dict:
    seeds = jax.random.split(jax.random.key(seed), 5)
    x_in = bell_draw(seeds[0], (CIN, NX, NY, NZ), 1.0, 6.0, ((0, 64), (1, 16)))
    weight = noise_with(seeds[1], (COUT, 27, CIN), (27 * CIN) ** -0.5, 0.21875, ((0, 64),), (0, 2, 64, 4.0))
    bias_vec = bell_draw(seeds[2], (COUT,), 0.5, 3.0, ((0, 64),))
    grad_out = bell_draw(seeds[3], (COUT, NX, NY, NZ), 1.0, 6.0, ((0, 64), (1, 16)))
    return dict(x_in=x_in, weight=weight, bias_vec=bias_vec, grad_out=grad_out)


def tap_list():
    return [(9 * i + 3 * j + l, i, j, l) for i in range(3) for j in range(3) for l in range(3)]

def reference(x_in, weight, bias_vec, grad_out):
    in_total = x_in.shape[0]
    out_total = weight.shape[0]
    n_cells = NX * NY * NZ
    pre_act = jnp.zeros((out_total, n_cells), jnp.float32) + bias_vec.astype(jnp.float32)[:, None]
    for k, i, j, l in tap_list():
        moved = jnp.roll(x_in, (1 - i, 1 - j, 1 - l), axis=(1, 2, 3)).reshape(in_total, n_cells)
        pre_act = pre_act + jnp.dot(weight[:, k, :], moved, preferred_element_type=jnp.float32)
    sigmoid_v = jax.nn.sigmoid(pre_act)
    activation = (pre_act * sigmoid_v).astype(jnp.bfloat16)
    slope = sigmoid_v * (1.0 + pre_act * (1.0 - sigmoid_v))
    grad_pre = (grad_out.reshape(out_total, n_cells).astype(jnp.float32) * slope).astype(jnp.bfloat16)
    grad_box = grad_pre.reshape(out_total, NX, NY, NZ)
    grad_scale = 1.0 / math.sqrt(n_cells)
    input_sum = jnp.zeros((in_total, n_cells), jnp.float32)
    filter_list = []
    for k, i, j, l in tap_list():
        back = jnp.roll(grad_box, (i - 1, j - 1, l - 1), axis=(1, 2, 3)).reshape(out_total, n_cells)
        input_sum = input_sum + jnp.dot(weight[:, k, :].T, back, preferred_element_type=jnp.float32)
        moved = jnp.roll(x_in, (1 - i, 1 - j, 1 - l), axis=(1, 2, 3)).reshape(in_total, n_cells)
        filter_list.append(lax.dot_general(grad_pre, moved, (((1,), (1,)), ((), ())), preferred_element_type=jnp.float32))
    weight_grad = jnp.stack(filter_list, axis=1) * grad_scale
    bias_grad = grad_scale * lax.optimization_barrier(jnp.sum(grad_pre.astype(jnp.float32), axis=1))
    return (activation.reshape(out_total, NX, NY, NZ), input_sum.astype(jnp.bfloat16).reshape(in_total, NX, NY, NZ), weight_grad, bias_grad)
```

```python
import functools
import math

import jax
import jax.numpy as jnp
from jax import lax
from jax.experimental import pallas as pl
from jax.experimental.pallas import tpu as pltpu
from jax.sharding import PartitionSpec as P

MESH = pl.DeviceIdType.MESH
F32, BF16 = jnp.float32, jnp.bfloat16
NX, NZ, NK = 4, 8, 2
NY, NH = 4, 4
NT = (((1,), (1,)), ((), ()))


class Copies:
    def __init__(self, send_sems):
        self.send_sems = send_sems
        self.started = []

    def send(self, src, dst, recv_sem, device):
        copy = pltpu.make_async_remote_copy(
            src_ref=src,
            dst_ref=dst,
            send_sem=self.send_sems.at[len(self.started)],
            recv_sem=recv_sem,
            device_id=device,
            device_id_type=MESH,
        )
        copy.start()
        self.started.append(copy)

    def drain(self):
        for copy in self.started:
            copy.wait_send()


def landed(dst, recv_sem):
    here = (lax.axis_index("slab"), lax.axis_index("chan"))
    pltpu.make_async_remote_copy(
        src_ref=dst, dst_ref=dst, send_sem=recv_sem, recv_sem=recv_sem, device_id=here, device_id_type=MESH
    ).wait_recv()


class Gather:
    def __init__(self, copies, place, buf, rz, rx, rc, rh):
        self.c = copies
        self.slab, self.x, self.z, self.k = place
        self.h, self.z4 = self.z // 4, self.z % 4
        self.mates = [(self.z4 + m) % 4 for m in range(1, 4)]
        self.buf, self.rz, self.rx, self.rc, self.rh = buf, rz, rx, rc, rh

    def dev(self, x, z, k):
        return (self.slab, (x * NZ + z) * NK + k)

    def borders(self):
        me = (self.x * NZ + self.z) * NK + self.k
        after, before = (self.slab + 1) % (NY * NH), (self.slab + NY * NH - 1) % (NY * NH)
        own = lambda q, p: self.buf.at[q, p, self.x, self.h, self.z4, self.k]
        self.c.send(own(0, 1), own(1, 0), self.rh.at[0], (after, me))
        self.c.send(own(0, 0), own(1, 1), self.rh.at[1], (before, me))

    def wait_borders(self):
        for side in range(2):
            landed(self.buf.at[1, side, self.x, self.h, self.z4, self.k], self.rh.at[side])

    def block(self, q, h, z4):
        return self.buf.at[q, :, self.x, h, z4, self.k]

    def piece(self, q, x, h, k):
        return self.buf.at[q, :, x, h, :, k]

    def z_send(self, q):
        mine = self.block(q, self.h, self.z4)
        for mate in self.mates:
            self.c.send(mine, mine, self.rz.at[q, self.z], self.dev(self.x, self.h * 4 + mate, self.k))
        self.c.send(mine, mine, self.rz.at[q, self.z], self.dev(self.x, (1 - self.h) * 4 + self.z4, self.k))

    def z_mates(self, q):
        for mate in self.mates:
            landed(self.block(q, self.h, mate), self.rz.at[q, self.h * 4 + mate])

    def z_mirror(self, q):
        other = (1 - self.h) * 4 + self.z4
        theirs = self.block(q, 1 - self.h, self.z4)
        landed(theirs, self.rz.at[q, other])
        for mate in self.mates:
            self.c.send(theirs, theirs, self.rz.at[q, other], self.dev(self.x, self.h * 4 + mate, self.k))

    def z_far(self, q):
        for mate in self.mates:
            landed(self.block(q, 1 - self.h, mate), self.rz.at[q, (1 - self.h) * 4 + mate])

    def c_send(self, q, x, h):
        mine = self.piece(q, x, h, self.k)
        self.c.send(mine, mine, self.rc.at[q, h, x], self.dev(self.x, self.z, 1 - self.k))

    def x_send(self, q, h):
        mine = self.piece(q, self.x, h, self.k)
        for step in (1, 3):
            self.c.send(mine, mine, self.rx.at[q, h, self.x], self.dev((self.x + step) % 4, self.z, self.k))
        self.c_send(q, self.x, h)

    def x_near(self, q, h):
        for step in (1, 3):
            x = (self.x + step) % 4
            landed(self.piece(q, x, h, self.k), self.rx.at[q, h, x])
        source, target = (self.x + 3 + 2 * self.k) % 4, (self.x + 1 + 2 * self.k) % 4
        passed = self.piece(q, source, h, self.k)
        self.c.send(passed, passed, self.rx.at[q, h, source], self.dev(target, self.z, self.k))
        for step in (1, 3):
            self.c_send(q, (self.x + step) % 4, h)

    def x_far(self, q, h):
        x = (self.x + 2) % 4
        landed(self.piece(q, x, h, self.k), self.rx.at[q, h, x])
        self.c_send(q, x, h)

    def c_wait(self, q):
        for h in range(2):
            for x in range(4):
                landed(self.piece(q, x, h, 1 - self.k), self.rc.at[q, h, x])

    def plane(self, q, p):
        return self.buf[q, p].reshape(2048, 128)

    def pair(self, q):
        return jnp.concatenate([self.plane(q, 0), self.plane(q, 1)], axis=1)


def band_weights(expanded, out, row_of, sign):
    lane = lax.broadcasted_iota(jnp.int32, (8, 2048), 1)
    sub = lax.broadcasted_iota(jnp.int32, (8, 2048), 0)
    tap = (sign * (lane - sub) + 1) & 7

    def one(t):
        rows = [expanded[pl.ds(row_of(t, j), 1), :] for j in range(3)]
        return jnp.where(tap == 0, rows[0], jnp.where(tap == 1, rows[1], jnp.where(tap == 2, rows[2], 0.0)))

    def body(u, carry):
        both = jnp.concatenate([one(2 * u), one(2 * u + 1)], axis=0)
        out[pl.ds(pl.multiple_of(16 * u, 16), 16), :] = both.astype(BF16)
        return carry

    lax.fori_loop(0, 18, body, 0)


def kernel(
    scale,
    x_ref, w1_ref, w2_ref, bias_ref, go_ref,
    act_ref, ig_ref, wg_ref, bg_ref,
    xb, gb, rep, wide, wa, wb, dm, dw, yb, zb, tot,
    send_sems, xz, xx, xc, xh, gz, gx, gc, gh, sy, sz, sg,
):
    slab, chan = lax.axis_index("slab"), lax.axis_index("chan")
    y, zh = slab // NH, slab % NH
    x, z, k = chan // (NZ * NK), chan // NK % NZ, chan % NK
    place = (slab, x, z, k)
    copies = Copies(send_sems)
    gx_ = Gather(copies, place, xb, xz, xx, xc, xh)
    gg_ = Gather(copies, place, gb, gz, gx, gc, gh)
    h, f = gx_.h, 1 - gx_.h
    at = lambda yy, hh: (yy * NH + hh, chan)

    partners = [gx_.dev(x, z, 1 - k)]
    partners += [gx_.dev((x + s) % 4, z, k) for s in (1, 3)]
    partners += [gx_.dev(x, h * 4 + m, k) for m in gx_.mates] + [gx_.dev(x, f * 4 + gx_.z4, k)]
    partners += [at((y + m) % NY, zh) for m in range(1, NY)]
    partners += [at(y, (zh + s) % NH) for s in (1, NH - 1)]
    partners += [((slab + s) % (NY * NH), chan) for s in (1, NY * NH - 1)]
    barrier = pltpu.get_barrier_semaphore()
    for partner in partners:
        pl.semaphore_signal(barrier, inc=1, device_id=partner, device_id_type=MESH)

    for p in range(2):
        xb[0, p, x, h, gx_.z4, k] = x_ref[p]
    for n in range(8):
        row = lax.broadcasted_iota(jnp.int32, (256, 256), 0)
        col = lax.broadcasted_iota(jnp.int32, (256, 256), 1)
        rep[:, 256 * n : 256 * n + 256] = jnp.where(row == 32 * n + (col >> 3), 1.0, 0.0).astype(BF16)

    pl.semaphore_wait(barrier, len(partners))
    gx_.borders()
    gx_.z_send(0)

    for n in range(8):
        wide[0:108, 256 * n : 256 * n + 256] = jnp.dot(
            w1_ref[...], rep[:, 256 * n : 256 * n + 256], preferred_element_type=F32
        )
    band_weights(wide, wa, lambda t, j: t // 12 * 36 + j * 12 + t % 12, 1)

    gx_.z_mates(0)
    gx_.x_send(0, h)
    gx_.z_mirror(0)
    gx_.x_near(0, h)
    gx_.wait_borders()
    gx_.z_send(1)
    gx_.z_far(0)
    gx_.x_send(0, f)
    gx_.x_far(0, h)
    gx_.z_mates(1)
    gx_.x_send(1, h)
    gx_.z_mirror(1)
    gx_.x_near(0, f)
    gx_.x_far(0, f)
    gx_.x_near(1, h)
    gx_.z_far(1)
    gx_.x_send(1, f)
    gx_.x_far(1, h)

    for c in range(4):
        turned = w2_ref[c].astype(F32).T.astype(BF16)
        for n in range(8):
            total = jnp.zeros((32, 256), F32)
            for o in range(4):
                row = lax.broadcasted_iota(jnp.int32, (64, 256), 0)
                col = lax.broadcasted_iota(jnp.int32, (64, 256), 1)
                pick = jnp.where(row * 4 + o == 32 * n + (col >> 3), 1.0, 0.0).astype(BF16)
                total += jnp.dot(turned[32 * o : 32 * o + 32], pick, preferred_element_type=F32)
            wide[32 * c : 32 * c + 32, 256 * n : 256 * n + 256] = total
    band_weights(wide, wb, lambda t, j: t % 4 * 32 + t // 12 * 9 + j * 3 + t % 12 // 4, -1)

    gx_.x_near(1, f)
    gx_.x_far(1, f)
    gx_.c_wait(0)
    gx_.c_wait(1)

    own = jnp.dot(wa[...], gx_.pair(0), preferred_element_type=F32)
    rim = jnp.dot(wa[...], gx_.pair(1), preferred_element_type=F32)

    def part(value, i, l, o, p):
        base = ((i * 3 + l) * 4 + o) * 8
        return value[base : base + 8, 128 * p : 128 * p + 128]

    grads = []
    for p in range(2):
        row = []
        for o in range(4):
            pre = jnp.full((8, 128), bias_ref[o], F32)
            for l in range(3):
                if p == 0:
                    term = part(rim, 0, l, o, 0) + part(own, 1, l, o, 0) + part(own, 2, l, o, 1)
                else:
                    term = part(own, 0, l, o, 0) + part(own, 1, l, o, 1) + part(rim, 2, l, o, 1)
                pre += term if l == 1 else pltpu.roll(term, (1 - l) % 128, 1)
            sig = 1.0 / (1.0 + jnp.exp(-pre))
            act_ref[o, p] = (pre * sig).astype(BF16)
            row.append(go_ref[o, p].astype(F32) * (sig * (1.0 + pre * (1.0 - sig))))
        grads.append(jnp.concatenate(row, axis=0).astype(BF16))
        gb[0, p, x, h, gx_.z4, k] = grads[p]

    gg_.borders()
    gg_.z_send(0)

    plain = jnp.concatenate(grads, axis=1).astype(F32)
    left, right = plain[:, :128], plain[:, 128:]
    turns = []
    for l in range(3):
        both = plain
        if l != 1:
            both = jnp.concatenate([pltpu.roll(v, (l - 1) % 128, 1) for v in (left, right)], axis=1)
        turns.append(both)
    rolled = jnp.concatenate(turns, axis=0).astype(BF16)
    lane = lax.broadcasted_iota(jnp.int32, (8, 2048), 1)
    sub = lax.broadcasted_iota(jnp.int32, (8, 2048), 0)
    tap = (lane - sub + 1) & 7
    planes = ((1, 0), (0, 0), (0, 1), (1, 1))
    sums = []
    for i in range(3):
        right_side = jnp.concatenate([gx_.plane(*planes[i]), gx_.plane(*planes[i + 1])], axis=1)
        full = lax.dot_general(rolled, right_side, NT, preferred_element_type=F32).reshape(12, 8, 2048)
        for j in range(3):
            kept = jnp.where((tap == j)[None], full, 0.0)
            dm[96 * j : 96 * j + 96, :] = kept.reshape(96, 2048).astype(BF16)
        folded = lax.dot_general(dm[...], rep[...], NT, preferred_element_type=F32)
        sums.append(jnp.sum(folded.reshape(36, 8, 256), axis=1))
    per_o = jnp.sum(plain.reshape(4, 8, 256), axis=(1, 2), keepdims=True).reshape(4, 1)
    sums.append(jnp.broadcast_to(per_o, (4, 256)))
    sums.append(jnp.zeros((16, 256), F32))
    dw[...] = jnp.concatenate(sums, axis=0).reshape(4, 32, 256)
    for m in range(1, NY):
        copies.send(dw.at[(y + m) % NY], yb.at[y], sy.at[y], at((y + m) % NY, zh))

    gg_.z_mates(0)
    gg_.x_send(0, h)
    gg_.z_mirror(0)
    yb[y] = dw[y]
    for m in range(1, NY):
        landed(yb.at[(y + m) % NY], sy.at[(y + m) % NY])
    zb[zh] = (yb[0] + yb[1] + yb[2] + yb[3]).astype(BF16)
    for s in (1, NH - 1):
        copies.send(zb.at[zh], zb.at[zh], sz.at[zh], at(y, (zh + s) % NH))

    gg_.x_near(0, h)
    gg_.wait_borders()
    gg_.z_send(1)
    gg_.z_far(0)
    gg_.x_send(0, f)
    gg_.x_far(0, h)
    gg_.z_mates(1)
    gg_.x_send(1, h)
    gg_.z_mirror(1)
    gg_.x_near(0, f)
    for s in (1, NH - 1):
        landed(zb.at[(zh + s) % NH], sz.at[(zh + s) % NH])
    source, target = (zh + 3 + 2 * k) % NH, (zh + 1 + 2 * k) % NH
    copies.send(zb.at[source], zb.at[source], sz.at[source], at(y, target))
    gg_.x_far(0, f)
    gg_.x_near(1, h)
    gg_.z_far(1)
    gg_.x_send(1, f)
    gg_.x_far(1, h)
    gg_.x_near(1, f)
    gg_.c_wait(0)
    own2 = jnp.dot(wb[...], gg_.pair(0), preferred_element_type=F32)
    landed(zb.at[(zh + 2) % NH], sz.at[(zh + 2) % NH])
    total = zb[0].astype(F32) + zb[1].astype(F32) + zb[2].astype(F32) + zb[3].astype(F32)
    tot[y] = total * scale
    for m in range(1, NY):
        copies.send(tot.at[y], tot.at[y], sg.at[y], at((y + m) % NY, zh))
    gg_.x_far(1, f)
    gg_.c_wait(1)
    rim2 = jnp.dot(wb[...], gg_.pair(1), preferred_element_type=F32)
    for p in range(2):
        for c in range(4):
            out = jnp.zeros((8, 128), F32)
            for l in range(3):
                if p == 0:
                    term = part(own2, 0, l, c, 1) + part(own2, 1, l, c, 0) + part(rim2, 2, l, c, 0)
                else:
                    term = part(rim2, 0, l, c, 1) + part(own2, 1, l, c, 1) + part(own2, 2, l, c, 0)
                out += term if l == 1 else pltpu.roll(term, (l - 1) % 128, 1)
            ig_ref[c, p] = out.astype(BF16)
    for m in range(1, NY):
        landed(tot.at[(y + m) % NY], sg.at[(y + m) % NY])
    everything = tot[...].reshape(128, 256)
    for t in range(27):
        wg_ref[t] = everything[4 * t : 4 * t + 4]
    bg_ref[...] = everything[108:112, :128]
    copies.drain()


def on_device(x_in, weight, bias_vec, grad_out):
    n_cells = lax.axis_size("slab") * x_in.shape[1] * x_in.shape[2] * x_in.shape[3]
    scale = 1.0 / math.sqrt(n_cells)
    planes = jnp.transpose(x_in, (1, 0, 2, 3)).reshape(2, 32, 128)
    by_tap = jnp.transpose(weight, (1, 0, 2)).reshape(108, 256)
    turned = jnp.pad(weight, ((0, 0), (0, 5), (0, 0))).reshape(128, 256).T.reshape(64, 4, 128)
    turned = lax.all_to_all(turned, "chan", 0, 0, tiled=True)
    turned = jnp.transpose(turned, (1, 0, 2))
    dma = lambda *shape: pltpu.SemaphoreType.DMA(shape)
    gathered = pltpu.VMEM((2, 2, NX, 2, 4, NK, 32, 128), BF16)
    vmem = pl.BlockSpec(memory_space=pltpu.VMEM)
    act, grad_in, filters, bias_grad = pl.pallas_call(
        functools.partial(kernel, scale),
        out_shape=(
            jax.ShapeDtypeStruct((4, 2, 8, 128), BF16),
            jax.ShapeDtypeStruct((4, 2, 8, 128), BF16),
            jax.ShapeDtypeStruct((27, 4, 256), F32),
            jax.ShapeDtypeStruct((4, 128), F32),
        ),
        in_specs=[vmem, vmem, vmem, pl.BlockSpec(memory_space=pltpu.SMEM), vmem],
        out_specs=(vmem,) * 4,
        scratch_shapes=[
            gathered,
            gathered,
            pltpu.VMEM((256, 2048), BF16),
            pltpu.VMEM((128, 2048), F32),
            pltpu.VMEM((288, 2048), BF16),
            pltpu.VMEM((288, 2048), BF16),
            pltpu.VMEM((288, 2048), BF16),
            pltpu.VMEM((4, 32, 256), F32),
            pltpu.VMEM((4, 32, 256), F32),
            pltpu.VMEM((4, 32, 256), BF16),
            pltpu.VMEM((4, 32, 256), F32),
            dma(100),
            *([dma(2, 8), dma(2, 2, 4), dma(2, 2, 4), dma(2)] * 2),
            dma(4),
            dma(4),
            dma(4),
        ],
        compiler_params=pltpu.CompilerParams(collective_id=0, has_side_effects=True),
    )(planes, by_tap, turned, bias_vec.astype(F32), grad_out)
    return (act, grad_in, jnp.transpose(filters, (1, 0, 2)), bias_grad[:, 0])


def solution(mesh):
    placed = (
        P("chan", "slab", None, None),
        P("chan", None, None),
        P("chan"),
        P("chan", "slab", None, None),
    )
    return jax.shard_map(
        on_device,
        mesh=mesh,
        in_specs=placed,
        out_specs=(
            P("chan", "slab", None, None),
            P("chan", "slab", None, None),
            P("chan", None, None),
            P("chan"),
        ),
        check_vma=False,
    )
```

```python
import functools
import math

import jax
import jax.numpy as jnp
from jax import lax
from jax.experimental import pallas as pl
from jax.experimental.pallas import tpu as pltpu
from jax.sharding import PartitionSpec as P

MESH = pl.DeviceIdType.MESH
F32, BF16 = jnp.float32, jnp.bfloat16
NX, NZ, NK = 4, 8, 2
NY, NH = 4, 4
NT = (((1,), (1,)), ((), ()))


class Copies:
    def __init__(self, send_sems):
        self.send_sems = send_sems
        self.started = []

    def send(self, src, dst, recv_sem, device):
        copy = pltpu.make_async_remote_copy(
            src_ref=src,
            dst_ref=dst,
            send_sem=self.send_sems.at[len(self.started)],
            recv_sem=recv_sem,
            device_id=device,
            device_id_type=MESH,
        )
        copy.start()
        self.started.append(copy)

    def drain(self):
        for copy in self.started:
            copy.wait_send()


def landed(dst, recv_sem):
    here = (lax.axis_index("slab"), lax.axis_index("chan"))
    pltpu.make_async_remote_copy(
        src_ref=dst, dst_ref=dst, send_sem=recv_sem, recv_sem=recv_sem, device_id=here, device_id_type=MESH
    ).wait_recv()


class Gather:
    def __init__(self, copies, place, buf, rz, rx, rc, rh):
        self.c = copies
        self.slab, self.x, self.z, self.k = place
        self.h, self.z4 = self.z // 4, self.z % 4
        self.mates = [(self.z4 + m) % 4 for m in range(1, 4)]
        self.buf, self.rz, self.rx, self.rc, self.rh = buf, rz, rx, rc, rh

    def dev(self, x, z, k):
        return (self.slab, (x * NZ + z) * NK + k)

    def borders(self):
        me = (self.x * NZ + self.z) * NK + self.k
        after, before = (self.slab + 1) % (NY * NH), (self.slab + NY * NH - 1) % (NY * NH)
        own = lambda q, p: self.buf.at[q, p, self.x, self.h, self.z4, self.k]
        self.c.send(own(0, 1), own(1, 0), self.rh.at[0], (after, me))
        self.c.send(own(0, 0), own(1, 1), self.rh.at[1], (before, me))

    def wait_borders(self):
        for side in range(2):
            landed(self.buf.at[1, side, self.x, self.h, self.z4, self.k], self.rh.at[side])

    def block(self, q, h, z4):
        return self.buf.at[q, :, self.x, h, z4, self.k]

    def piece(self, q, x, h, k):
        return self.buf.at[q, :, x, h, :, k]

    def z_send(self, q):
        mine = self.block(q, self.h, self.z4)
        for mate in self.mates:
            self.c.send(mine, mine, self.rz.at[q, self.z], self.dev(self.x, self.h * 4 + mate, self.k))
        self.c.send(mine, mine, self.rz.at[q, self.z], self.dev(self.x, (1 - self.h) * 4 + self.z4, self.k))

    def z_mates(self, q):
        for mate in self.mates:
            landed(self.block(q, self.h, mate), self.rz.at[q, self.h * 4 + mate])

    def z_mirror(self, q):
        other = (1 - self.h) * 4 + self.z4
        theirs = self.block(q, 1 - self.h, self.z4)
        landed(theirs, self.rz.at[q, other])
        for mate in self.mates:
            self.c.send(theirs, theirs, self.rz.at[q, other], self.dev(self.x, self.h * 4 + mate, self.k))

    def z_far(self, q):
        for mate in self.mates:
            landed(self.block(q, 1 - self.h, mate), self.rz.at[q, (1 - self.h) * 4 + mate])

    def c_send(self, q, x, h):
        mine = self.piece(q, x, h, self.k)
        self.c.send(mine, mine, self.rc.at[q, h, x], self.dev(self.x, self.z, 1 - self.k))

    def x_send(self, q, h):
        mine = self.piece(q, self.x, h, self.k)
        for step in (1, 3):
            self.c.send(mine, mine, self.rx.at[q, h, self.x], self.dev((self.x + step) % 4, self.z, self.k))
        self.c_send(q, self.x, h)

    def x_near(self, q, h):
        for step in (1, 3):
            x = (self.x + step) % 4
            landed(self.piece(q, x, h, self.k), self.rx.at[q, h, x])
        source, target = (self.x + 3 + 2 * self.k) % 4, (self.x + 1 + 2 * self.k) % 4
        passed = self.piece(q, source, h, self.k)
        self.c.send(passed, passed, self.rx.at[q, h, source], self.dev(target, self.z, self.k))
        for step in (1, 3):
            self.c_send(q, (self.x + step) % 4, h)

    def x_far(self, q, h):
        x = (self.x + 2) % 4
        landed(self.piece(q, x, h, self.k), self.rx.at[q, h, x])
        self.c_send(q, x, h)

    def c_wait(self, q):
        for h in range(2):
            for x in range(4):
                landed(self.piece(q, x, h, 1 - self.k), self.rc.at[q, h, x])

    def plane(self, q, p):
        return self.buf[q, p].reshape(2048, 128)

    def pair(self, q):
        return jnp.concatenate([self.plane(q, 0), self.plane(q, 1)], axis=1)


def band_weights(expanded, out, row_of, sign):
    lane = lax.broadcasted_iota(jnp.int32, (8, 2048), 1)
    sub = lax.broadcasted_iota(jnp.int32, (8, 2048), 0)
    tap = (sign * (lane - sub) + 1) & 7

    def one(t):
        rows = [expanded[pl.ds(row_of(t, j), 1), :] for j in range(3)]
        return jnp.where(tap == 0, rows[0], jnp.where(tap == 1, rows[1], jnp.where(tap == 2, rows[2], 0.0)))

    def body(u, carry):
        both = jnp.concatenate([one(2 * u), one(2 * u + 1)], axis=0)
        out[pl.ds(pl.multiple_of(16 * u, 16), 16), :] = both.astype(BF16)
        return carry

    lax.fori_loop(0, 18, body, 0)


def turned_weights(all_rows, spread, wide, k):
    row = lax.broadcasted_iota(jnp.int32, (64, 256), 0)
    col = lax.broadcasted_iota(jnp.int32, (64, 256), 1)
    source = jnp.where(row < 32, 2 * row + k, 2 * row - 63 - k)
    within = lax.broadcasted_iota(jnp.int32, (27, 128), 1) // 8 % 4
    for c in range(4):
        low, high = [all_rows[pl.ds(4 * q + c, 64, stride=8), :] for q in range(2)]
        mine = jnp.where(k == 0, low, high).T.astype(BF16)
        for n in range(8):
            pick = jnp.where(source == 8 * n + (col >> 5), 1.0, 0.0).astype(BF16)
            full = jnp.dot(mine, pick, preferred_element_type=F32)
            for half in range(2):
                spread[2 * n + half] = full[:, 128 * half : 128 * half + 128]
                total = spread[2 * n + half, pl.ds(0, 27, stride=4), :]
                for o in range(1, 4):
                    total = jnp.where(within == o, spread[2 * n + half, pl.ds(o, 27, stride=4), :], total)
                wide[32 * c : 32 * c + 27, 256 * n + 128 * half : 256 * n + 128 * half + 128] = total


def kernel(
    scale,
    x_ref, w_ref, bias_ref, go_ref,
    act_ref, ig_ref, out_ref,
    xb, gb, rep, wide, spread, wa, wb, dm, rows, t1, t2, t3, t4, all_rows, dw, yb, zb, tot, po, pi,
    send_sems, xz, xx, xc, xh, gz, gx, gc, s1, s2, s3, sy, sz, sg, sp,
):
    slab, chan = lax.axis_index("slab"), lax.axis_index("chan")
    y, zh = slab // NH, slab % NH
    x, z, k = chan // (NZ * NK), chan // NK % NZ, chan % NK
    place = (slab, x, z, k)
    copies = Copies(send_sems)
    gx_ = Gather(copies, place, xb, xz, xx, xc, xh)
    gg_ = Gather(copies, place, gb, gz, gx, gc, None)
    h, f = gx_.h, 1 - gx_.h
    at = lambda yy, hh: (yy * NH + hh, chan)
    line = [(z + m) % NZ for m in range(1, NZ)]
    ring = [(x + m) % NX for m in range(1, NX)]
    after, before = ((slab + 1) % (NY * NH), chan), ((slab + NY * NH - 1) % (NY * NH), chan)

    partners = [gx_.dev(x, z, 1 - k)]
    partners += [gx_.dev(xx_, z, k) for xx_ in ring]
    partners += [gx_.dev(x, zz, k) for zz in line]
    partners += [at((y + m) % NY, zh) for m in range(1, NY)]
    partners += [at(y, (zh + s) % NH) for s in (1, NH - 1)]
    partners += [after, before]
    barrier = pltpu.get_barrier_semaphore()
    for partner in partners:
        pl.semaphore_signal(barrier, inc=1, device_id=partner, device_id_type=MESH)

    for p in range(2):
        xb[0, p, x, h, gx_.z4, k] = x_ref[:, p].astype(F32).reshape(32, 128).astype(BF16)
    rows[104:128, :] = jnp.zeros((24, 256), F32)
    for t in range(27):
        rows[4 * t : 4 * t + 4, :] = w_ref[t].astype(F32)
    t1[...] = rows[...].T.reshape(4, 8, 8, 128).astype(BF16)
    for n in range(8):
        row = lax.broadcasted_iota(jnp.int32, (256, 256), 0)
        col = lax.broadcasted_iota(jnp.int32, (256, 256), 1)
        rep[:, 256 * n : 256 * n + 256] = jnp.where(row == 32 * n + (col >> 3), 1.0, 0.0).astype(BF16)
    by_tap = rows[...].astype(BF16)
    for n in range(8):
        wide[:, 256 * n : 256 * n + 256] = jnp.dot(
            by_tap, rep[:, 256 * n : 256 * n + 256], preferred_element_type=F32
        )
    band_weights(wide, wa, lambda t, j: t // 12 * 36 + j * 12 + t % 12, 1)

    pl.semaphore_wait(barrier, len(partners))
    gx_.borders()
    gx_.z_send(0)
    for zz in line:
        copies.send(t1.at[:, zz], t2.at[z], s1.at[z], gx_.dev(x, zz, k))
    t2[z] = t1[:, z]

    gx_.z_mates(0)
    gx_.x_send(0, h)
    gx_.z_mirror(0)
    gx_.x_near(0, h)
    gx_.z_far(0)
    gx_.x_send(0, f)
    gx_.wait_borders()
    gx_.z_send(1)
    gx_.x_far(0, h)
    for zz in line:
        landed(t2.at[zz], s1.at[zz])
    for xx_ in ring:
        copies.send(t2.at[:, xx_], t3.at[x], s2.at[x], gx_.dev(xx_, z, k))
    t3[x] = t2[:, x]
    gx_.z_mates(1)
    gx_.x_send(1, h)
    gx_.z_mirror(1)
    gx_.x_near(0, f)
    gx_.x_near(1, h)
    gx_.x_far(0, f)
    gx_.z_far(1)
    gx_.x_send(1, f)
    gx_.x_far(1, h)
    for xx_ in ring:
        landed(t3.at[xx_], s2.at[xx_])
    copies.send(t3, t4, s3, gx_.dev(x, z, 1 - k))
    gx_.x_near(1, f)
    gx_.x_far(1, f)
    gx_.c_wait(0)
    gx_.c_wait(1)

    own = jnp.dot(wa[...], gx_.pair(0), preferred_element_type=F32)
    rim = jnp.dot(wa[...], gx_.pair(1), preferred_element_type=F32)

    def part(value, i, l, o, p):
        base = ((i * 3 + l) * 4 + o) * 8
        return value[base : base + 8, 128 * p : 128 * p + 128]

    def turned_sum(terms, sign):
        total = None
        for l in range(3):
            term = terms(l)
            term = term if l == 1 else pltpu.roll(term, sign * (1 - l) % 128, 1)
            total = term if total is None else total + term
        return total

    offsets = bias_ref[...].astype(F32)
    grads = []
    for p in range(2):
        row = []
        for o in range(4):
            if p == 0:
                terms = lambda l: part(rim, 0, l, o, 0) + part(own, 1, l, o, 0) + part(own, 2, l, o, 1)
            else:
                terms = lambda l: part(own, 0, l, o, 0) + part(own, 1, l, o, 1) + part(rim, 2, l, o, 1)
            pre = turned_sum(terms, 1) + offsets[:, o : o + 1]
            sig = 1.0 / (1.0 + jnp.exp(-pre))
            act_ref[o, p] = (pre * sig).astype(BF16)
            row.append(go_ref[o, p].astype(F32) * (sig * (1.0 + pre * (1.0 - sig))))
        grads.append(jnp.concatenate(row, axis=0).astype(BF16))
        gb[0, p, x, h, gx_.z4, k] = grads[p]

    gg_.z_send(0)

    plain = jnp.concatenate(grads, axis=1).astype(F32)
    left, right = plain[:, :128], plain[:, 128:]
    turns = []
    for l in range(3):
        both = plain
        if l != 1:
            both = jnp.concatenate([pltpu.roll(v, (l - 1) % 128, 1) for v in (left, right)], axis=1)
        turns.append(both)
    rolled = jnp.concatenate(turns, axis=0).astype(BF16)
    lane = lax.broadcasted_iota(jnp.int32, (8, 2048), 1)
    sub = lax.broadcasted_iota(jnp.int32, (8, 2048), 0)
    tap = (lane - sub + 1) & 7
    planes = ((1, 0), (0, 0), (0, 1), (1, 1))
    sums = []
    for i in range(3):
        right_side = jnp.concatenate([gx_.plane(*planes[i]), gx_.plane(*planes[i + 1])], axis=1)
        full = lax.dot_general(rolled, right_side, NT, preferred_element_type=F32).reshape(12, 8, 2048)
        for j in range(3):
            kept = jnp.where((tap == j)[None], full, 0.0)
            dm[96 * j : 96 * j + 96, :] = kept.reshape(96, 2048).astype(BF16)
        folded = lax.dot_general(dm[...], rep[...], NT, preferred_element_type=F32)
        sums.append(jnp.sum(folded.reshape(36, 8, 256), axis=1))
    per_o = jnp.sum(plain.reshape(4, 8, 256), axis=(1, 2), keepdims=True).reshape(4, 1)
    sums.append(jnp.broadcast_to(per_o, (4, 256)))
    sums.append(jnp.zeros((16, 256), F32))
    dw[...] = jnp.concatenate(sums, axis=0).reshape(4, 32, 256).astype(BF16)
    for m in range(1, NY):
        copies.send(dw.at[(y + m) % NY], yb.at[y], sy.at[y], at((y + m) % NY, zh))

    gg_.z_mates(0)
    gg_.x_send(0, h)
    gg_.z_mirror(0)
    yb[y] = dw[y]
    for m in range(1, NY):
        landed(yb.at[(y + m) % NY], sy.at[(y + m) % NY])
    zb[zh] = sum(yb[m].astype(F32) for m in range(NY)).astype(BF16)
    for s in (1, NH - 1):
        copies.send(zb.at[zh], zb.at[zh], sz.at[zh], at(y, (zh + s) % NH))

    gg_.x_near(0, h)
    gg_.z_far(0)
    gg_.x_send(0, f)

    landed(t4, s3)
    all_rows[0:256, :] = t3[...].astype(F32).reshape(256, 128)
    all_rows[256:512, :] = t4[...].astype(F32).reshape(256, 128)
    turned_weights(all_rows, spread, wide, k)
    band_weights(wide, wb, lambda t, j: t % 4 * 32 + t // 12 * 9 + j * 3 + t % 12 // 4, -1)

    gg_.x_far(0, h)
    gg_.x_near(0, f)
    for s in (1, NH - 1):
        landed(zb.at[(zh + s) % NH], sz.at[(zh + s) % NH])
    source, target = (zh + 3 + 2 * k) % NH, (zh + 1 + 2 * k) % NH
    copies.send(zb.at[source], zb.at[source], sz.at[source], at(y, target))
    gg_.x_far(0, f)
    gg_.c_wait(0)
    own2 = jnp.dot(wb[...], gg_.pair(0), preferred_element_type=F32)
    for c in range(4):
        po[0, c] = turned_sum(lambda l: part(own2, 2, l, c, 1), -1).astype(BF16)
        po[1, c] = turned_sum(lambda l: part(own2, 0, l, c, 0), -1).astype(BF16)
    copies.send(po.at[0], pi.at[0], sp.at[0], after)
    copies.send(po.at[1], pi.at[1], sp.at[1], before)
    landed(zb.at[(zh + 2) % NH], sz.at[(zh + 2) % NH])
    tot[y] = sum(zb[m].astype(F32) for m in range(NH)) * scale
    for m in range(1, NY):
        copies.send(tot.at[y], tot.at[y], sg.at[y], at((y + m) % NY, zh))
    for p in range(2):
        landed(pi.at[p], sp.at[p])
        for c in range(4):
            if p == 0:
                terms = lambda l: part(own2, 0, l, c, 1) + part(own2, 1, l, c, 0)
            else:
                terms = lambda l: part(own2, 1, l, c, 1) + part(own2, 2, l, c, 0)
            ig_ref[c, p] = (turned_sum(terms, -1) + pi[p, c].astype(F32)).astype(BF16)
    for m in range(1, NY):
        landed(tot.at[(y + m) % NY], sg.at[(y + m) % NY])
    out_ref[...] = tot[...].reshape(128, 256)
    copies.drain()


def finish(act_in, ig_in, sums, act_ref, ig_ref, wg_ref, bg_ref):
    act_ref[...] = act_in[...]
    ig_ref[...] = ig_in[...]
    for t in range(27):
        wg_ref[t] = sums[4 * t : 4 * t + 4, :]
    tail = sums[104:112, 0:128]
    lane = lax.broadcasted_iota(jnp.int32, (8, 128), 1)
    sub = lax.broadcasted_iota(jnp.int32, (8, 128), 0)
    bg_ref[...] = jnp.sum(jnp.where(sub == lane + 4, tail, 0.0), axis=0, keepdims=True)[:, 0:4]


def on_device(x_in, weight, bias_vec, grad_out):
    n_cells = lax.axis_size("slab") * x_in.shape[1] * x_in.shape[2] * x_in.shape[3]
    scale = 1.0 / math.sqrt(n_cells)
    dma = lambda *shape: pltpu.SemaphoreType.DMA(shape)
    vmem = pl.BlockSpec(memory_space=pltpu.VMEM)
    block = jax.ShapeDtypeStruct((4, 2, 8, 128), BF16)
    act, grad_in, sums = pl.pallas_call(
        functools.partial(kernel, scale),
        out_shape=(block, block, jax.ShapeDtypeStruct((128, 256), F32)),
        in_specs=[vmem] * 4,
        out_specs=(vmem,) * 3,
        scratch_shapes=[
            pltpu.VMEM((2, 2, NX, 2, 4, NK, 32, 128), BF16),
            pltpu.VMEM((1, 2, NX, 2, 4, NK, 32, 128), BF16),
            pltpu.VMEM((256, 2048), BF16),
            pltpu.VMEM((128, 2048), F32),
            pltpu.VMEM((16, 128, 128), F32),
            pltpu.VMEM((288, 2048), BF16),
            pltpu.VMEM((288, 2048), BF16),
            pltpu.VMEM((288, 2048), BF16),
            pltpu.VMEM((128, 256), F32),
            pltpu.VMEM((NX, NZ, 8, 128), BF16),
            pltpu.VMEM((NZ, NX, 8, 128), BF16),
            pltpu.VMEM((NX, NZ, 8, 128), BF16),
            pltpu.VMEM((NX, NZ, 8, 128), BF16),
            pltpu.VMEM((512, 128), F32),
            pltpu.VMEM((4, 32, 256), BF16),
            pltpu.VMEM((4, 32, 256), BF16),
            pltpu.VMEM((4, 32, 256), BF16),
            pltpu.VMEM((4, 32, 256), F32),
            pltpu.VMEM((2, 4, 8, 128), BF16),
            pltpu.VMEM((2, 4, 8, 128), BF16),
            dma(96),
            dma(2, 8), dma(2, 2, 4), dma(2, 2, 4), dma(2),
            dma(1, 8), dma(1, 2, 4), dma(1, 2, 4),
            dma(8), dma(4), pltpu.SemaphoreType.DMA,
            dma(4), dma(4), dma(4), dma(2),
        ],
        compiler_params=pltpu.CompilerParams(collective_id=0, has_side_effects=True),
    )(x_in, jnp.transpose(weight, (1, 0, 2)), bias_vec.reshape(1, 4), grad_out)
    act, grad_in, filters, bias_grad = pl.pallas_call(
        finish,
        out_shape=(
            block,
            block,
            jax.ShapeDtypeStruct((27, 4, 256), F32),
            jax.ShapeDtypeStruct((1, 4), F32),
        ),
        in_specs=[vmem] * 3,
        out_specs=(vmem,) * 4,
    )(act, grad_in, sums)
    return (act, grad_in, jnp.transpose(filters, (1, 0, 2)), bias_grad.reshape(4))


def solution(mesh):
    placed = (
        P("chan", "slab", None, None),
        P("chan", None, None),
        P("chan"),
        P("chan", "slab", None, None),
    )
    return jax.shard_map(
        on_device,
        mesh=mesh,
        in_specs=placed,
        out_specs=(
            P("chan", "slab", None, None),
            P("chan", "slab", None, None),
            P("chan", None, None),
            P("chan"),
        ),
        check_vma=False,
    )
```

```python
import functools
import math

import jax
import jax.numpy as jnp
from jax import lax
from jax.experimental import pallas as pl
from jax.experimental.pallas import tpu as pltpu
from jax.sharding import PartitionSpec as P

MESH = pl.DeviceIdType.MESH
F32, BF16 = jnp.float32, jnp.bfloat16
NX, NZ, NK = 4, 8, 2
NY, NH = 4, 4
NT = (((1,), (1,)), ((), ()))


class Copies:
    def __init__(self, send_sems):
        self.send_sems = send_sems
        self.started = []

    def send(self, src, dst, recv_sem, device):
        copy = pltpu.make_async_remote_copy(
            src_ref=src,
            dst_ref=dst,
            send_sem=self.send_sems.at[len(self.started)],
            recv_sem=recv_sem,
            device_id=device,
            device_id_type=MESH,
        )
        copy.start()
        self.started.append(copy)

    def drain(self):
        for copy in self.started:
            copy.wait_send()


def landed(dst, recv_sem):
    here = (lax.axis_index("slab"), lax.axis_index("chan"))
    pltpu.make_async_remote_copy(
        src_ref=dst, dst_ref=dst, send_sem=recv_sem, recv_sem=recv_sem, device_id=here, device_id_type=MESH
    ).wait_recv()


class Gather:
    def __init__(self, copies, place, buf, rz, rx, rc):
        self.c = copies
        self.slab, self.x, self.z, self.k = place
        self.h, self.z4 = self.z // 4, self.z % 4
        self.f = 1 - self.h
        self.mates = [(self.z4 + m) % 4 for m in range(1, 4)]
        self.near_x = [(self.x + step) % 4 for step in (1, 3)]
        self.far_x = (self.x + 2) % 4
        self.buf, self.rz, self.rx, self.rc = buf, rz, rx, rc

    def dev(self, x, z, k):
        return (self.slab, (x * NZ + z) * NK + k)

    def block(self, x, h, z4, k):
        return self.buf.at[:, x, h, z4, k]

    def unit(self, x, z4, k):
        if z4 is None:
            return self.buf.at[:, x, self.h, :, k], 4
        return self.buf.at[:, x, self.f, z4, k], z4

    def z_send(self):
        mine = self.block(self.x, self.h, self.z4, self.k)
        for mate in self.mates:
            self.c.send(mine, mine, self.rz.at[self.z], self.dev(self.x, self.h * 4 + mate, self.k))
        self.c.send(mine, mine, self.rz.at[self.z], self.dev(self.x, self.f * 4 + self.z4, self.k))

    def z_mates(self):
        for mate in self.mates:
            landed(self.block(self.x, self.h, mate, self.k), self.rz.at[self.h * 4 + mate])
        self.x_send(None)

    def z_mirror(self):
        other = self.f * 4 + self.z4
        theirs = self.block(self.x, self.f, self.z4, self.k)
        landed(theirs, self.rz.at[other])
        for mate in self.mates:
            self.c.send(theirs, theirs, self.rz.at[other], self.dev(self.x, self.h * 4 + mate, self.k))
        self.x_send(self.z4)

    def z_far(self):
        for mate in self.mates:
            landed(self.block(self.x, self.f, mate, self.k), self.rz.at[self.f * 4 + mate])
            self.x_send(mate)

    def c_send(self, x, z4):
        mine, at = self.unit(x, z4, self.k)
        self.c.send(mine, mine, self.rc.at[at, x], self.dev(self.x, self.z, 1 - self.k))

    def x_send(self, z4):
        mine, at = self.unit(self.x, z4, self.k)
        for x in self.near_x:
            self.c.send(mine, mine, self.rx.at[at, self.x], self.dev(x, self.z, self.k))
        self.c_send(self.x, z4)

    def x_near(self, z4):
        for x in self.near_x:
            theirs, at = self.unit(x, z4, self.k)
            landed(theirs, self.rx.at[at, x])
        source, target = (self.x + 3 + 2 * self.k) % 4, (self.x + 1 + 2 * self.k) % 4
        passed, at = self.unit(source, z4, self.k)
        self.c.send(passed, passed, self.rx.at[at, source], self.dev(target, self.z, self.k))
        for x in self.near_x:
            self.c_send(x, z4)

    def x_far(self, z4):
        theirs, at = self.unit(self.far_x, z4, self.k)
        landed(theirs, self.rx.at[at, self.far_x])
        self.c_send(self.far_x, z4)

    def c_wait(self):
        for z4 in (None, self.z4, *self.mates):
            for x in range(4):
                theirs, at = self.unit(x, z4, 1 - self.k)
                landed(theirs, self.rc.at[at, x])

    def pair(self):
        return jnp.concatenate([self.buf[p].reshape(2048, 128) for p in range(2)], axis=1)


def band_weights(expanded, out, row_of, sign):
    lane = lax.broadcasted_iota(jnp.int32, (8, 2048), 1)
    sub = lax.broadcasted_iota(jnp.int32, (8, 2048), 0)
    tap = (sign * (lane - sub) + 1) & 7

    def one(t):
        rows = [expanded[pl.ds(row_of(t, j), 1), :] for j in range(3)]
        return jnp.where(tap == 0, rows[0], jnp.where(tap == 1, rows[1], jnp.where(tap == 2, rows[2], 0.0)))

    def body(u, carry):
        both = jnp.concatenate([one(2 * u), one(2 * u + 1)], axis=0)
        out[pl.ds(pl.multiple_of(16 * u, 16), 16), :] = both.astype(BF16)
        return carry

    lax.fori_loop(0, 18, body, 0)


def turned_weights(all_rows, spread, wide, k):
    row = lax.broadcasted_iota(jnp.int32, (64, 256), 0)
    col = lax.broadcasted_iota(jnp.int32, (64, 256), 1)
    source = jnp.where(row < 32, 2 * row + k, 2 * row - 63 - k)
    within = lax.broadcasted_iota(jnp.int32, (27, 128), 1) // 8 % 4
    for c in range(4):
        low, high = [all_rows[pl.ds(4 * q + c, 64, stride=8), :] for q in range(2)]
        mine = jnp.where(k == 0, low, high).T.astype(BF16)
        for n in range(8):
            pick = jnp.where(source == 8 * n + (col >> 5), 1.0, 0.0).astype(BF16)
            full = jnp.dot(mine, pick, preferred_element_type=F32)
            for half in range(2):
                spread[2 * n + half] = full[:, 128 * half : 128 * half + 128]
                total = spread[2 * n + half, pl.ds(0, 27, stride=4), :]
                for o in range(1, 4):
                    total = jnp.where(within == o, spread[2 * n + half, pl.ds(o, 27, stride=4), :], total)
                wide[32 * c : 32 * c + 27, 256 * n + 128 * half : 256 * n + 128 * half + 128] = total


def kernel(
    scale,
    x_hbm, w_hbm, bias_hbm, go_hbm,
    act_ref, ig_ref, out_ref,
    x_ref, w_ref, bias_ref, go_ref, load_sems,
    xb, gb, rep, wide, spread, wa, wb, dm, rows, t1, t2, t3, t4, all_rows, dw, yb, zb, tot, po, pi, fo, fi, go_rim,
    send_sems, xz, xx, xc, gz, gx, gc, s1, s2, s3, sy, sz, sg, sp, sf, so,
):
    slab, chan = lax.axis_index("slab"), lax.axis_index("chan")
    y, zh = slab // NH, slab % NH
    x, z, k = chan // (NZ * NK), chan // NK % NZ, chan % NK
    place = (slab, x, z, k)
    copies = Copies(send_sems)
    gx_ = Gather(copies, place, xb, xz, xx, xc)
    gg_ = Gather(copies, place, gb, gz, gx, gc)
    h = gx_.h
    at = lambda yy, hh: (yy * NH + hh, chan)
    line = [(z + m) % NZ for m in range(1, NZ)]
    ring = [(x + m) % NX for m in range(1, NX)]
    after, before = ((slab + 1) % (NY * NH), chan), ((slab + NY * NH - 1) % (NY * NH), chan)

    partners = [gx_.dev(x, z, 1 - k)]
    partners += [gx_.dev(xx_, z, k) for xx_ in ring]
    partners += [gx_.dev(x, zz, k) for zz in line]
    partners += [at((y + m) % NY, zh) for m in range(1, NY)]
    partners += [at(y, (zh + s) % NH) for s in (1, NH - 1)]
    partners += [after, before]
    barrier = pltpu.get_barrier_semaphore()
    for partner in partners:
        pl.semaphore_signal(barrier, inc=1, device_id=partner, device_id_type=MESH)

    loads = [
        pltpu.make_async_copy(source, target, load_sems.at[n])
        for n, (source, target) in enumerate(
            ((w_hbm, w_ref), (x_hbm, x_ref), (go_hbm, go_ref), (bias_hbm, bias_ref))
        )
    ]
    for load in loads:
        load.start()
    for n in range(8):
        row = lax.broadcasted_iota(jnp.int32, (256, 256), 0)
        col = lax.broadcasted_iota(jnp.int32, (256, 256), 1)
        rep[:, 256 * n : 256 * n + 256] = jnp.where(row == 32 * n + (col >> 3), 1.0, 0.0).astype(BF16)
    for load in loads:
        load.wait()
    for p in range(2):
        xb[p, x, h, gx_.z4, k] = x_ref[:, p].astype(F32).reshape(32, 128).astype(BF16)
    rows[104:128, :] = jnp.zeros((24, 256), F32)
    for t in range(27):
        rows[4 * t : 4 * t + 4, :] = w_ref[t].astype(F32)
    t1[...] = rows[...].T.reshape(4, 8, 8, 128).astype(BF16)
    by_tap = rows[...].astype(BF16)
    for n in range(8):
        wide[:, 256 * n : 256 * n + 256] = jnp.dot(
            by_tap, rep[:, 256 * n : 256 * n + 256], preferred_element_type=F32
        )
    band_weights(wide, wa, lambda t, j: t // 12 * 36 + j * 12 + t % 12, 1)

    pl.semaphore_wait(barrier, len(partners))
    gx_.z_send()
    gx_.z_mates()
    gx_.z_mirror()
    gx_.x_near(None)
    gx_.z_far()
    copies.send(go_ref.at[:, 1], go_rim.at[0], so.at[0], after)
    copies.send(go_ref.at[:, 0], go_rim.at[1], so.at[1], before)
    for zz in line:
        copies.send(t1.at[:, zz], t2.at[z], s1.at[z], gx_.dev(x, zz, k))
    t2[z] = t1[:, z]
    gx_.x_near(gx_.z4)
    gx_.x_far(None)
    for mate in gx_.mates:
        gx_.x_near(mate)
    gx_.x_far(gx_.z4)
    for mate in gx_.mates:
        gx_.x_far(mate)
    gx_.c_wait()

    own = jnp.dot(wa[...], gx_.pair(), preferred_element_type=F32)

    def part(value, i, l, o, p):
        base = ((i * 3 + l) * 4 + o) * 8
        return value[base : base + 8, 128 * p : 128 * p + 128]

    def turned_sum(terms, sign):
        total = None
        for l in range(3):
            term = terms(l)
            term = term if l == 1 else pltpu.roll(term, sign * (1 - l) % 128, 1)
            total = term if total is None else total + term
        return total

    shares = [
        [turned_sum(lambda l: part(own, 2, l, o, 0), 1) for o in range(4)],
        [turned_sum(lambda l: part(own, 1, l, o, 0) + part(own, 2, l, o, 1), 1) for o in range(4)],
        [turned_sum(lambda l: part(own, 0, l, o, 0) + part(own, 1, l, o, 1), 1) for o in range(4)],
        [turned_sum(lambda l: part(own, 0, l, o, 1), 1) for o in range(4)],
    ]
    for o in range(4):
        for n in range(4):
            fo[n, o] = shares[n][o].astype(BF16)
    copies.send(fo.at[2:4], fi.at[0:2], sf.at[0], after)
    copies.send(fo.at[0:2], fi.at[2:4], sf.at[1], before)

    for zz in line:
        landed(t2.at[zz], s1.at[zz])
    for xx_ in ring:
        copies.send(t2.at[:, xx_], t3.at[x], s2.at[x], gx_.dev(xx_, z, k))
    t3[x] = t2[:, x]
    for xx_ in ring:
        landed(t3.at[xx_], s2.at[xx_])
    copies.send(t3, t4, s3, gx_.dev(x, z, 1 - k))
    landed(t4, s3)
    all_rows[0:256, :] = t3[...].astype(F32).reshape(256, 128)
    all_rows[256:512, :] = t4[...].astype(F32).reshape(256, 128)
    turned_weights(all_rows, spread, wide, k)
    band_weights(wide, wb, lambda t, j: t % 4 * 32 + t // 12 * 9 + j * 3 + t % 12 // 4, -1)

    landed(fi.at[0:2], sf.at[0])
    landed(fi.at[2:4], sf.at[1])
    for side in range(2):
        landed(go_rim.at[side], so.at[side])
    offsets = bias_ref[...].astype(F32)
    grads = []
    for n in range(4):
        row = []
        for o in range(4):
            pre = shares[n][o] + fi[n, o].astype(F32) + offsets[:, o : o + 1]
            sig = 1.0 / (1.0 + jnp.exp(-pre))
            if n in (1, 2):
                act_ref[o, n - 1] = (pre * sig).astype(BF16)
                given = go_ref[o, n - 1]
            else:
                given = go_rim[n // 3, o]
            row.append(given.astype(F32) * (sig * (1.0 + pre * (1.0 - sig))))
        grads.append(jnp.concatenate(row, axis=0).astype(BF16))
    gb[0, x, h, gx_.z4, k] = grads[1]
    gb[1, x, h, gx_.z4, k] = grads[2]

    gg_.z_send()

    grads = [g.astype(F32) for g in grads]
    turns = [[g if l == 1 else pltpu.roll(g, (l - 1) % 128, 1) for l in range(3)] for g in grads]
    rolled = jnp.concatenate(
        [jnp.concatenate([turns[2 - i][l], turns[3 - i][l]], axis=1) for i in range(3) for l in range(3)], axis=0
    ).astype(BF16)
    lane = lax.broadcasted_iota(jnp.int32, (8, 2048), 1)
    sub = lax.broadcasted_iota(jnp.int32, (8, 2048), 0)
    tap = (lane - sub + 1) & 7
    whole = lax.dot_general(rolled, gx_.pair(), NT, preferred_element_type=F32)
    sums = []
    for i in range(3):
        full = whole[96 * i : 96 * i + 96].reshape(12, 8, 2048)
        for j in range(3):
            kept = jnp.where((tap == j)[None], full, 0.0)
            dm[96 * j : 96 * j + 96, :] = kept.reshape(96, 2048).astype(BF16)
        folded = lax.dot_general(dm[...], rep[...], NT, preferred_element_type=F32)
        sums.append(jnp.sum(folded.reshape(36, 8, 256), axis=1))
    per_o = jnp.sum((grads[1] + grads[2]).reshape(4, 8, 128), axis=(1, 2), keepdims=True).reshape(4, 1)
    sums.append(jnp.broadcast_to(per_o, (4, 256)))
    sums.append(jnp.zeros((16, 256), F32))
    dw[...] = jnp.concatenate(sums, axis=0).reshape(4, 32, 256).astype(BF16)
    for m in range(1, NY):
        copies.send(dw.at[(y + m) % NY], yb.at[y], sy.at[y], at((y + m) % NY, zh))

    gg_.z_mates()
    gg_.z_mirror()
    yb[y] = dw[y]
    for m in range(1, NY):
        landed(yb.at[(y + m) % NY], sy.at[(y + m) % NY])
    zb[zh] = sum(yb[m].astype(F32) for m in range(NY)).astype(BF16)
    for s in (1, NH - 1):
        copies.send(zb.at[zh], zb.at[zh], sz.at[zh], at(y, (zh + s) % NH))

    gg_.x_near(None)
    gg_.z_far()
    gg_.x_near(gg_.z4)
    gg_.x_far(None)
    for mate in gg_.mates:
        gg_.x_near(mate)
    for s in (1, NH - 1):
        landed(zb.at[(zh + s) % NH], sz.at[(zh + s) % NH])
    source, target = (zh + 3 + 2 * k) % NH, (zh + 1 + 2 * k) % NH
    copies.send(zb.at[source], zb.at[source], sz.at[source], at(y, target))
    gg_.x_far(gg_.z4)
    for mate in gg_.mates:
        gg_.x_far(mate)
    gg_.c_wait()
    own2 = jnp.dot(wb[...], gg_.pair(), preferred_element_type=F32)
    for c in range(4):
        po[0, c] = turned_sum(lambda l: part(own2, 2, l, c, 1), -1).astype(BF16)
        po[1, c] = turned_sum(lambda l: part(own2, 0, l, c, 0), -1).astype(BF16)
    copies.send(po.at[0], pi.at[0], sp.at[0], after)
    copies.send(po.at[1], pi.at[1], sp.at[1], before)
    landed(zb.at[(zh + 2) % NH], sz.at[(zh + 2) % NH])
    tot[y] = sum(zb[m].astype(F32) for m in range(NH)) * scale
    for m in range(1, NY):
        copies.send(tot.at[y], tot.at[y], sg.at[y], at((y + m) % NY, zh))
    for p in range(2):
        landed(pi.at[p], sp.at[p])
        for c in range(4):
            if p == 0:
                terms = lambda l: part(own2, 0, l, c, 1) + part(own2, 1, l, c, 0)
            else:
                terms = lambda l: part(own2, 1, l, c, 1) + part(own2, 2, l, c, 0)
            ig_ref[c, p] = (turned_sum(terms, -1) + pi[p, c].astype(F32)).astype(BF16)
    for m in range(1, NY):
        landed(tot.at[(y + m) % NY], sg.at[(y + m) % NY])
    out_ref[...] = tot[...].reshape(128, 256)
    copies.drain()


def finish(act_in, ig_in, sums, act_ref, ig_ref, wg_ref, bg_ref):
    act_ref[...] = act_in[...]
    ig_ref[...] = ig_in[...]
    for t in range(27):
        wg_ref[t] = sums[4 * t : 4 * t + 4, :]
    tail = sums[104:112, 0:128]
    lane = lax.broadcasted_iota(jnp.int32, (8, 128), 1)
    sub = lax.broadcasted_iota(jnp.int32, (8, 128), 0)
    bg_ref[...] = jnp.sum(jnp.where(sub == lane + 4, tail, 0.0), axis=0, keepdims=True)[:, 0:4]


def on_device(x_in, weight, bias_vec, grad_out):
    n_cells = lax.axis_size("slab") * x_in.shape[1] * x_in.shape[2] * x_in.shape[3]
    scale = 1.0 / math.sqrt(n_cells)
    dma = lambda *shape: pltpu.SemaphoreType.DMA(shape)
    vmem, anywhere = pl.BlockSpec(memory_space=pltpu.VMEM), pl.BlockSpec(memory_space=pl.ANY)
    held = lambda *args: pltpu.with_memory_space_constraint(*args, pltpu.VMEM)
    block = jax.ShapeDtypeStruct((4, 2, 8, 128), BF16)
    act, grad_in, sums = pl.pallas_call(
        functools.partial(kernel, scale),
        out_shape=(
            pltpu.VMEM((4, 2, 8, 128), BF16),
            pltpu.VMEM((4, 2, 8, 128), BF16),
            pltpu.VMEM((128, 256), F32),
        ),
        in_specs=[anywhere] * 4,
        out_specs=(vmem,) * 3,
        scratch_shapes=[
            pltpu.VMEM((4, 2, 8, 128), BF16),
            pltpu.VMEM((27, 4, 256), BF16),
            pltpu.VMEM((1, 4), BF16),
            pltpu.VMEM((4, 2, 8, 128), BF16),
            dma(4),
            pltpu.VMEM((2, NX, 2, 4, NK, 32, 128), BF16),
            pltpu.VMEM((2, NX, 2, 4, NK, 32, 128), BF16),
            pltpu.VMEM((256, 2048), BF16),
            pltpu.VMEM((128, 2048), F32),
            pltpu.VMEM((16, 128, 128), F32),
            pltpu.VMEM((288, 2048), BF16),
            pltpu.VMEM((288, 2048), BF16),
            pltpu.VMEM((288, 2048), BF16),
            pltpu.VMEM((128, 256), F32),
            pltpu.VMEM((NX, NZ, 8, 128), BF16),
            pltpu.VMEM((NZ, NX, 8, 128), BF16),
            pltpu.VMEM((NX, NZ, 8, 128), BF16),
            pltpu.VMEM((NX, NZ, 8, 128), BF16),
            pltpu.VMEM((512, 128), F32),
            pltpu.VMEM((4, 32, 256), BF16),
            pltpu.VMEM((4, 32, 256), BF16),
            pltpu.VMEM((4, 32, 256), BF16),
            pltpu.VMEM((4, 32, 256), F32),
            pltpu.VMEM((2, 4, 8, 128), BF16),
            pltpu.VMEM((2, 4, 8, 128), BF16),
            pltpu.VMEM((4, 4, 8, 128), BF16),
            pltpu.VMEM((4, 4, 8, 128), BF16),
            pltpu.VMEM((2, 4, 8, 128), BF16),
            dma(120),
            dma(8), dma(5, 4), dma(5, 4),
            dma(8), dma(5, 4), dma(5, 4),
            dma(8), dma(4), pltpu.SemaphoreType.DMA,
            dma(4), dma(4), dma(4), dma(2), dma(2), dma(2),
        ],
        compiler_params=pltpu.CompilerParams(collective_id=0, has_side_effects=True),
    )(x_in, jnp.transpose(weight, (1, 0, 2)), bias_vec.reshape(1, 4), grad_out)
    act, grad_in, filters, bias_grad = pl.pallas_call(
        finish,
        out_shape=(
            block,
            block,
            jax.ShapeDtypeStruct((27, 4, 256), F32),
            jax.ShapeDtypeStruct((1, 4), F32),
        ),
        in_specs=[vmem] * 3,
        out_specs=(vmem,) * 4,
    )(held(act), held(grad_in), held(sums))
    return (act, grad_in, jnp.transpose(filters, (1, 0, 2)), bias_grad.reshape(4))


def solution(mesh):
    placed = (
        P("chan", "slab", None, None),
        P("chan", None, None),
        P("chan"),
        P("chan", "slab", None, None),
    )
    return jax.shard_map(
        on_device,
        mesh=mesh,
        in_specs=placed,
        out_specs=(
            P("chan", "slab", None, None),
            P("chan", "slab", None, None),
            P("chan", None, None),
            P("chan"),
        ),
        check_vma=False,
    )
```

```python
import functools
import math

import jax
import jax.numpy as jnp
from jax import lax
from jax.experimental import pallas as pl
from jax.experimental.pallas import tpu as pltpu
from jax.sharding import PartitionSpec as P

MESH = pl.DeviceIdType.MESH
F32, BF16 = jnp.float32, jnp.bfloat16
NX, NZ, NK = 4, 8, 2
NY, NH = 4, 4
NT = (((1,), (1,)), ((), ()))


class Copies:
    def __init__(self, send_sems):
        self.send_sems = send_sems
        self.started = []

    def send(self, src, dst, recv_sem, device):
        copy = pltpu.make_async_remote_copy(
            src_ref=src,
            dst_ref=dst,
            send_sem=self.send_sems.at[len(self.started)],
            recv_sem=recv_sem,
            device_id=device,
            device_id_type=MESH,
        )
        copy.start()
        self.started.append(copy)

    def drain(self):
        for copy in self.started:
            copy.wait_send()
        self.started = []


def landed(dst, recv_sem):
    here = (lax.axis_index("slab"), lax.axis_index("chan"))
    pltpu.make_async_remote_copy(
        src_ref=dst, dst_ref=dst, send_sem=recv_sem, recv_sem=recv_sem, device_id=here, device_id_type=MESH
    ).wait_recv()


class Gather:
    def __init__(self, copies, place, buf, rz, rn, rf, rc):
        self.c = copies
        self.slab, self.x, self.z, self.k = place
        self.h, self.z4 = self.z // 4, self.z % 4
        self.f = 1 - self.h
        self.mates = [(self.z4 + m) % 4 for m in range(1, 4)]
        self.near_x = [(self.x + step) % 4 for step in (1, 3)]
        self.far_x = (self.x + 2) % 4
        self.buf, self.rz, self.rn, self.rf, self.rc = buf, rz, rn, rf, rc

    def dev(self, x, z, k):
        return (self.slab, (x * NZ + z) * NK + k)

    def block(self, x, h, z4, k):
        return self.buf.at[:, x, h, z4, k]

    def half(self, x, h, k):
        return self.buf.at[:, x, h, :, k]

    def unit(self, x, z4):
        if z4 is None:
            return self.half(x, self.h, self.k), 4
        return self.block(x, self.f, z4, self.k), z4

    def z_send(self):
        mine = self.block(self.x, self.h, self.z4, self.k)
        for mate in self.mates:
            self.c.send(mine, mine, self.rz.at[self.z], self.dev(self.x, self.h * 4 + mate, self.k))
        self.c.send(mine, mine, self.rz.at[self.z], self.dev(self.x, self.f * 4 + self.z4, self.k))

    def z_mates(self):
        for mate in self.mates:
            landed(self.block(self.x, self.h, mate, self.k), self.rz.at[self.h * 4 + mate])
        self.x_send(None)
        self.c_send(self.x, self.h)

    def z_mirror(self):
        other = self.f * 4 + self.z4
        theirs = self.block(self.x, self.f, self.z4, self.k)
        landed(theirs, self.rz.at[other])
        for mate in self.mates:
            self.c.send(theirs, theirs, self.rz.at[other], self.dev(self.x, self.h * 4 + mate, self.k))
        self.x_send(self.z4)

    def z_far(self):
        for mate in self.mates:
            landed(self.block(self.x, self.f, mate, self.k), self.rz.at[self.f * 4 + mate])
            self.x_send(mate)
        self.c_send(self.x, self.f)

    def c_send(self, x, h):
        mine = self.half(x, h, self.k)
        self.c.send(mine, mine, self.rc, self.dev(self.x, self.z, 1 - self.k))

    def x_send(self, z4):
        mine, at = self.unit(self.x, z4)
        for way, x in enumerate(self.near_x):
            self.c.send(mine, mine, self.rn.at[at, way], self.dev(x, self.z, self.k))

    def x_near(self, z4):
        for way, x in enumerate(self.near_x):
            theirs, at = self.unit(x, z4)
            landed(theirs, self.rn.at[at, 1 - way])
        source, target = (self.x + 3 + 2 * self.k) % 4, (self.x + 1 + 2 * self.k) % 4
        passed, _ = self.unit(source, z4)
        self.c.send(passed, passed, self.rf.at[0 if z4 is None else 1], self.dev(target, self.z, self.k))

    def near_to_core(self, h):
        for x in self.near_x:
            self.c_send(x, h)

    def x_far(self, n):
        h = (self.h, self.f)[n]
        landed(self.half(self.far_x, h, self.k), self.rf.at[n])
        self.c_send(self.far_x, h)

    def c_wait(self):
        landed(self.buf.at[:, :, :, :, 1 - self.k], self.rc)

    def pair(self):
        return jnp.concatenate([self.buf[p].reshape(2048, 128) for p in range(2)], axis=1)


def band_weights(expanded, out, row_of, sign):
    lane = lax.broadcasted_iota(jnp.int32, (8, 2048), 1)
    sub = lax.broadcasted_iota(jnp.int32, (8, 2048), 0)
    tap = (sign * (lane - sub) + 1) & 7

    def one(t):
        rows = [expanded[pl.ds(row_of(t, j), 1), :] for j in range(3)]
        return jnp.where(tap == 0, rows[0], jnp.where(tap == 1, rows[1], jnp.where(tap == 2, rows[2], 0.0)))

    def body(u, carry):
        both = jnp.concatenate([one(2 * u), one(2 * u + 1)], axis=0)
        out[pl.ds(pl.multiple_of(16 * u, 16), 16), :] = both.astype(BF16)
        return carry

    lax.fori_loop(0, 18, body, 0)


def turned_weights(all_rows, spread, wide, k):
    row = lax.broadcasted_iota(jnp.int32, (64, 256), 0)
    col = lax.broadcasted_iota(jnp.int32, (64, 256), 1)
    source = jnp.where(row < 32, 2 * row + k, 2 * row - 63 - k)
    within = lax.broadcasted_iota(jnp.int32, (27, 128), 1) // 8 % 4
    for c in range(4):
        low, high = [all_rows[pl.ds(4 * q + c, 64, stride=8), :] for q in range(2)]
        mine = jnp.where(k == 0, low, high).T.astype(BF16)
        for n in range(8):
            pick = jnp.where(source == 8 * n + (col >> 5), 1.0, 0.0).astype(BF16)
            full = jnp.dot(mine, pick, preferred_element_type=F32)
            for half in range(2):
                spread[2 * n + half] = full[:, 128 * half : 128 * half + 128]
                total = spread[2 * n + half, pl.ds(0, 27, stride=4), :]
                for o in range(1, 4):
                    total = jnp.where(within == o, spread[2 * n + half, pl.ds(o, 27, stride=4), :], total)
                wide[32 * c : 32 * c + 27, 256 * n + 128 * half : 256 * n + 128 * half + 128] = total


def kernel(
    scale,
    x_hbm, w_hbm, bias_hbm, go_hbm,
    act_ref, ig_ref, out_ref,
    x_ref, w_ref, bias_ref, go_ref, load_sems,
    xb, gb, rep, wide, spread, wa, wb, dm, rows, t1, t2, t3, t4, all_rows, dw, yb, zb, tot, po, pi, fo, fi, go_rim,
    send_sems, xz, xn, xf, xc, gz, gn, gf, gc, s1, s2, s3, sy, sz, sg, sp, sf, so, ready,
):
    slab, chan = lax.axis_index("slab"), lax.axis_index("chan")
    y, zh = slab // NH, slab % NH
    x, z, k = chan // (NZ * NK), chan // NK % NZ, chan % NK
    place = (slab, x, z, k)
    copies = Copies(send_sems)
    gx_ = Gather(copies, place, xb, xz, xn, xf, xc)
    gg_ = Gather(copies, place, gb, gz, gn, gf, gc)
    h = gx_.h
    at = lambda yy, hh: (yy * NH + hh, chan)
    line = [(z + m) % NZ for m in range(1, NZ)]
    ring = [(x + m) % NX for m in range(1, NX)]
    after, before = ((slab + 1) % (NY * NH), chan), ((slab + NY * NH - 1) % (NY * NH), chan)

    def signal(sem, device):
        pl.semaphore_signal(sem, inc=1, device_id=device, device_id_type=MESH)

    partners = [gx_.dev(x, z, 1 - k)]
    partners += [gx_.dev(xx_, z, k) for xx_ in ring]
    partners += [gx_.dev(x, h * 4 + m, k) for m in gx_.mates] + [gx_.dev(x, gx_.f * 4 + gx_.z4, k)]
    partners += [at((y + m) % NY, zh) for m in range(1, NY)]
    barrier = pltpu.get_barrier_semaphore()
    for partner in partners:
        signal(barrier, partner)
    greets = {0: [at(y, 1), at(y, 3), at((y + NY - 1) % NY, 3)], 1: [at(y, 2)], 3: [at(y, 2)]}
    answers = {1: [at(y, 0)], 2: [at(y, 1), at(y, 3)], 3: [at(y, 0), at((y + 1) % NY, 0)]}
    for who, devices in greets.items():

        @pl.when(zh == who)
        def _(devices=devices):
            for device in devices:
                signal(barrier, device)

    loads = [
        pltpu.make_async_copy(source, target, load_sems.at[n])
        for n, (source, target) in enumerate(
            ((w_hbm, w_ref), (x_hbm, x_ref), (go_hbm, go_ref), (bias_hbm, bias_ref))
        )
    ]
    for load in loads:
        load.start()
    for n in range(8):
        row = lax.broadcasted_iota(jnp.int32, (256, 256), 0)
        col = lax.broadcasted_iota(jnp.int32, (256, 256), 1)
        rep[:, 256 * n : 256 * n + 256] = jnp.where(row == 32 * n + (col >> 3), 1.0, 0.0).astype(BF16)
    for load in loads:
        load.wait()
    for p in range(2):
        xb[p, x, h, gx_.z4, k] = x_ref[:, p].astype(F32).reshape(32, 128).astype(BF16)
    rows[104:128, :] = jnp.zeros((24, 256), F32)
    for t in range(27):
        rows[4 * t : 4 * t + 4, :] = w_ref[t].astype(F32)
    t1[...] = rows[...].T.reshape(4, 8, 8, 128).astype(BF16)
    by_tap = rows[...].astype(BF16)
    for n in range(8):
        wide[:, 256 * n : 256 * n + 256] = jnp.dot(
            by_tap, rep[:, 256 * n : 256 * n + 256], preferred_element_type=F32
        )
    band_weights(wide, wa, lambda t, j: t // 12 * 36 + j * 12 + t % 12, 1)

    pl.semaphore_wait(barrier, len(partners) + jnp.where(zh == 0, 0, jnp.where(zh == 1, 1, 2)))
    for who, devices in answers.items():

        @pl.when(zh == who)
        def _(devices=devices):
            for device in devices:
                signal(ready, device)

    gx_.z_send()
    gx_.z_mates()
    gx_.z_mirror()
    gx_.x_near(None)
    gx_.near_to_core(h)
    gx_.z_far()
    for zz in line:
        copies.send(t1.at[:, zz], t2.at[z], s1.at[z], gx_.dev(x, zz, k))
    t2[z] = t1[:, z]
    gx_.x_near(gx_.z4)
    gx_.x_far(0)
    for mate in gx_.mates:
        gx_.x_near(mate)
    gx_.near_to_core(gx_.f)
    gx_.x_far(1)

    for who, devices in greets.items():

        @pl.when(zh == who)
        def _(devices=devices):
            pl.semaphore_wait(ready, len(devices))

    copies.send(go_ref.at[:, 1], go_rim.at[0], so.at[0], after)
    copies.send(go_ref.at[:, 0], go_rim.at[1], so.at[1], before)
    gx_.c_wait()

    own = jnp.dot(wa[...], gx_.pair(), preferred_element_type=F32)

    def part(value, i, l, o, p):
        base = ((i * 3 + l) * 4 + o) * 8
        return value[base : base + 8, 128 * p : 128 * p + 128]

    def turned_sum(terms, sign):
        total = None
        for l in range(3):
            term = terms(l)
            term = term if l == 1 else pltpu.roll(term, sign * (1 - l) % 128, 1)
            total = term if total is None else total + term
        return total

    shares = [
        [turned_sum(lambda l: part(own, 2, l, o, 0), 1) for o in range(4)],
        [turned_sum(lambda l: part(own, 1, l, o, 0) + part(own, 2, l, o, 1), 1) for o in range(4)],
        [turned_sum(lambda l: part(own, 0, l, o, 0) + part(own, 1, l, o, 1), 1) for o in range(4)],
        [turned_sum(lambda l: part(own, 0, l, o, 1), 1) for o in range(4)],
    ]
    for o in range(4):
        for n in range(4):
            fo[n, o] = shares[n][o].astype(BF16)
    copies.send(fo.at[2:4], fi.at[0:2], sf.at[0], after)
    copies.send(fo.at[0:2], fi.at[2:4], sf.at[1], before)

    for zz in line:
        landed(t2.at[zz], s1.at[zz])
    for xx_ in ring:
        copies.send(t2.at[:, xx_], t3.at[x], s2.at[x], gx_.dev(xx_, z, k))
    t3[x] = t2[:, x]
    for xx_ in ring:
        landed(t3.at[xx_], s2.at[xx_])
    copies.send(t3, t4, s3, gx_.dev(x, z, 1 - k))
    landed(t4, s3)
    all_rows[0:256, :] = t3[...].astype(F32).reshape(256, 128)
    all_rows[256:512, :] = t4[...].astype(F32).reshape(256, 128)
    turned_weights(all_rows, spread, wide, k)
    band_weights(wide, wb, lambda t, j: t % 4 * 32 + t // 12 * 9 + j * 3 + t % 12 // 4, -1)

    landed(fi.at[0:2], sf.at[0])
    landed(fi.at[2:4], sf.at[1])
    for side in range(2):
        landed(go_rim.at[side], so.at[side])
    copies.drain()
    offsets = bias_ref[...].astype(F32)
    grads = []
    for n in range(4):
        row = []
        for o in range(4):
            pre = shares[n][o] + fi[n, o].astype(F32) + offsets[:, o : o + 1]
            sig = 1.0 / (1.0 + jnp.exp(-pre))
            if n in (1, 2):
                act_ref[o, n - 1] = (pre * sig).astype(BF16)
                given = go_ref[o, n - 1]
            else:
                given = go_rim[n // 3, o]
            row.append(given.astype(F32) * (sig * (1.0 + pre * (1.0 - sig))))
        grads.append(jnp.concatenate(row, axis=0).astype(BF16))
    gb[0, x, h, gx_.z4, k] = grads[1]
    gb[1, x, h, gx_.z4, k] = grads[2]

    gg_.z_send()

    grads = [g.astype(F32) for g in grads]
    turns = [[g if l == 1 else pltpu.roll(g, (l - 1) % 128, 1) for l in range(3)] for g in grads]
    rolled = jnp.concatenate(
        [jnp.concatenate([turns[2 - i][l], turns[3 - i][l]], axis=1) for i in range(3) for l in range(3)], axis=0
    ).astype(BF16)
    lane = lax.broadcasted_iota(jnp.int32, (8, 2048), 1)
    sub = lax.broadcasted_iota(jnp.int32, (8, 2048), 0)
    tap = (lane - sub + 1) & 7
    whole = lax.dot_general(rolled, gx_.pair(), NT, preferred_element_type=F32)
    sums = []
    for i in range(3):
        full = whole[96 * i : 96 * i + 96].reshape(12, 8, 2048)
        for j in range(3):
            kept = jnp.where((tap == j)[None], full, 0.0)
            dm[96 * j : 96 * j + 96, :] = kept.reshape(96, 2048).astype(BF16)
        folded = lax.dot_general(dm[...], rep[...], NT, preferred_element_type=F32)
        sums.append(jnp.sum(folded.reshape(36, 8, 256), axis=1))
    per_o = jnp.sum((grads[1] + grads[2]).reshape(4, 8, 128), axis=(1, 2), keepdims=True).reshape(4, 1)
    sums.append(jnp.broadcast_to(per_o, (4, 256)))
    sums.append(jnp.zeros((16, 256), F32))
    dw[...] = jnp.concatenate(sums, axis=0).reshape(4, 32, 256).astype(BF16)
    for m in range(1, NY):
        copies.send(dw.at[(y + m) % NY], yb.at[y], sy.at[y], at((y + m) % NY, zh))

    gg_.z_mates()
    gg_.z_mirror()
    yb[y] = dw[y]
    for m in range(1, NY):
        landed(yb.at[(y + m) % NY], sy.at[(y + m) % NY])
    zb[zh] = sum(yb[m].astype(F32) for m in range(NY)).astype(BF16)
    for s in (1, NH - 1):
        copies.send(zb.at[zh], zb.at[zh], sz.at[zh], at(y, (zh + s) % NH))

    gg_.x_near(None)
    gg_.near_to_core(h)
    gg_.z_far()
    gg_.x_near(gg_.z4)
    gg_.x_far(0)
    for mate in gg_.mates:
        gg_.x_near(mate)
    gg_.near_to_core(gg_.f)
    for s in (1, NH - 1):
        landed(zb.at[(zh + s) % NH], sz.at[(zh + s) % NH])
    source, target = (zh + 3 + 2 * k) % NH, (zh + 1 + 2 * k) % NH
    copies.send(zb.at[source], zb.at[source], sz.at[source], at(y, target))
    gg_.x_far(1)
    gg_.c_wait()
    own2 = jnp.dot(wb[...], gg_.pair(), preferred_element_type=F32)
    for c in range(4):
        po[0, c] = turned_sum(lambda l: part(own2, 2, l, c, 1), -1).astype(BF16)
        po[1, c] = turned_sum(lambda l: part(own2, 0, l, c, 0), -1).astype(BF16)
    copies.send(po.at[0], pi.at[0], sp.at[0], after)
    copies.send(po.at[1], pi.at[1], sp.at[1], before)
    landed(zb.at[(zh + 2) % NH], sz.at[(zh + 2) % NH])
    tot[y] = sum(zb[m].astype(F32) for m in range(NH)) * scale
    for m in range(1, NY):
        copies.send(tot.at[y], tot.at[y], sg.at[y], at((y + m) % NY, zh))
    for p in range(2):
        landed(pi.at[p], sp.at[p])
        for c in range(4):
            if p == 0:
                terms = lambda l: part(own2, 0, l, c, 1) + part(own2, 1, l, c, 0)
            else:
                terms = lambda l: part(own2, 1, l, c, 1) + part(own2, 2, l, c, 0)
            ig_ref[c, p] = (turned_sum(terms, -1) + pi[p, c].astype(F32)).astype(BF16)
    for m in range(1, NY):
        landed(tot.at[(y + m) % NY], sg.at[(y + m) % NY])
    out_ref[...] = tot[...].reshape(128, 256)
    copies.drain()


def finish(act_in, ig_in, sums, act_ref, ig_ref, wg_ref, bg_ref):
    act_ref[...] = act_in[...]
    ig_ref[...] = ig_in[...]
    for t in range(27):
        wg_ref[t] = sums[4 * t : 4 * t + 4, :]
    tail = sums[104:112, 0:128]
    lane = lax.broadcasted_iota(jnp.int32, (8, 128), 1)
    sub = lax.broadcasted_iota(jnp.int32, (8, 128), 0)
    bg_ref[...] = jnp.sum(jnp.where(sub == lane + 4, tail, 0.0), axis=0, keepdims=True)[:, 0:4]


def on_device(x_in, weight, bias_vec, grad_out):
    n_cells = lax.axis_size("slab") * x_in.shape[1] * x_in.shape[2] * x_in.shape[3]
    scale = 1.0 / math.sqrt(n_cells)
    dma = lambda *shape: pltpu.SemaphoreType.DMA(shape)
    vmem, anywhere = pl.BlockSpec(memory_space=pltpu.VMEM), pl.BlockSpec(memory_space=pl.ANY)
    held = lambda *args: pltpu.with_memory_space_constraint(*args, pltpu.VMEM)
    block = jax.ShapeDtypeStruct((4, 2, 8, 128), BF16)
    act, grad_in, sums = pl.pallas_call(
        functools.partial(kernel, scale),
        out_shape=(
            pltpu.VMEM((4, 2, 8, 128), BF16),
            pltpu.VMEM((4, 2, 8, 128), BF16),
            pltpu.VMEM((128, 256), F32),
        ),
        in_specs=[anywhere] * 4,
        out_specs=(vmem,) * 3,
        scratch_shapes=[
            pltpu.VMEM((4, 2, 8, 128), BF16),
            pltpu.VMEM((27, 4, 256), BF16),
            pltpu.VMEM((1, 4), BF16),
            pltpu.VMEM((4, 2, 8, 128), BF16),
            dma(4),
            pltpu.VMEM((2, NX, 2, 4, NK, 32, 128), BF16),
            pltpu.VMEM((2, NX, 2, 4, NK, 32, 128), BF16),
            pltpu.VMEM((256, 2048), BF16),
            pltpu.VMEM((128, 2048), F32),
            pltpu.VMEM((16, 128, 128), F32),
            pltpu.VMEM((288, 2048), BF16),
            pltpu.VMEM((288, 2048), BF16),
            pltpu.VMEM((288, 2048), BF16),
            pltpu.VMEM((128, 256), F32),
            pltpu.VMEM((NX, NZ, 8, 128), BF16),
            pltpu.VMEM((NZ, NX, 8, 128), BF16),
            pltpu.VMEM((NX, NZ, 8, 128), BF16),
            pltpu.VMEM((NX, NZ, 8, 128), BF16),
            pltpu.VMEM((512, 128), F32),
            pltpu.VMEM((4, 32, 256), BF16),
            pltpu.VMEM((4, 32, 256), BF16),
            pltpu.VMEM((4, 32, 256), BF16),
            pltpu.VMEM((4, 32, 256), F32),
            pltpu.VMEM((2, 4, 8, 128), BF16),
            pltpu.VMEM((2, 4, 8, 128), BF16),
            pltpu.VMEM((4, 4, 8, 128), BF16),
            pltpu.VMEM((4, 4, 8, 128), BF16),
            pltpu.VMEM((2, 4, 8, 128), BF16),
            dma(48),
            dma(8), dma(5, 2), dma(2), pltpu.SemaphoreType.DMA,
            dma(8), dma(5, 2), dma(2), pltpu.SemaphoreType.DMA,
            dma(8), dma(4), pltpu.SemaphoreType.DMA,
            dma(4), dma(4), dma(4), dma(2), dma(2), dma(2),
            pltpu.SemaphoreType.REGULAR,
        ],
        compiler_params=pltpu.CompilerParams(collective_id=0, has_side_effects=True),
    )(x_in, jnp.transpose(weight, (1, 0, 2)), bias_vec.reshape(1, 4), grad_out)
    act, grad_in, filters, bias_grad = pl.pallas_call(
        finish,
        out_shape=(
            block,
            block,
            jax.ShapeDtypeStruct((27, 4, 256), F32),
            jax.ShapeDtypeStruct((1, 4), F32),
        ),
        in_specs=[vmem] * 3,
        out_specs=(vmem,) * 4,
    )(held(act), held(grad_in), held(sums))
    return (act, grad_in, jnp.transpose(filters, (1, 0, 2)), bias_grad.reshape(4))


def solution(mesh):
    placed = (
        P("chan", "slab", None, None),
        P("chan", None, None),
        P("chan"),
        P("chan", "slab", None, None),
    )
    return jax.shard_map(
        on_device,
        mesh=mesh,
        in_specs=placed,
        out_specs=(
            P("chan", "slab", None, None),
            P("chan", "slab", None, None),
            P("chan", None, None),
            P("chan"),
        ),
        check_vma=False,
    )
```

```python
import functools
import math

import jax
import jax.numpy as jnp
from jax import lax
from jax.experimental import pallas as pl
from jax.experimental.pallas import tpu as pltpu
from jax.sharding import PartitionSpec as P

MESH = pl.DeviceIdType.MESH
F32, BF16 = jnp.float32, jnp.bfloat16
NX, NZ, NK = 4, 8, 2
NY, NH = 4, 4
NT = (((1,), (1,)), ((), ()))


class Copies:
    def __init__(self, send_sems):
        self.send_sems = send_sems
        self.started = []

    def send(self, src, dst, recv_sem, device):
        copy = pltpu.make_async_remote_copy(
            src_ref=src,
            dst_ref=dst,
            send_sem=self.send_sems.at[len(self.started)],
            recv_sem=recv_sem,
            device_id=device,
            device_id_type=MESH,
        )
        copy.start()
        self.started.append(copy)

    def drain(self):
        for copy in self.started:
            copy.wait_send()
        self.started = []


def landed(dst, recv_sem):
    here = (lax.axis_index("slab"), lax.axis_index("chan"))
    pltpu.make_async_remote_copy(
        src_ref=dst, dst_ref=dst, send_sem=recv_sem, recv_sem=recv_sem, device_id=here, device_id_type=MESH
    ).wait_recv()


class Gather:
    def __init__(self, copies, place, buf, rz, rn, rf, rc):
        self.c = copies
        self.slab, self.x, self.z, self.k = place
        self.h, self.z4 = self.z // 4, self.z % 4
        self.f = 1 - self.h
        self.mates = [(self.z4 + m) % 4 for m in range(1, 4)]
        self.near_x = [(self.x + step) % 4 for step in (1, 3)]
        self.far_x = (self.x + 2) % 4
        self.buf, self.rz, self.rn, self.rf, self.rc = buf, rz, rn, rf, rc

    def dev(self, x, z, k):
        return (self.slab, (x * NZ + z) * NK + k)

    def block(self, x, h, z4, k):
        return self.buf.at[:, x, h, z4, k]

    def half(self, x, h, k):
        return self.buf.at[:, x, h, :, k]

    def unit(self, x, z4):
        if z4 is None:
            return self.half(x, self.h, self.k), 4
        return self.block(x, self.f, z4, self.k), z4

    def z_send(self):
        mine = self.block(self.x, self.h, self.z4, self.k)
        for mate in self.mates:
            self.c.send(mine, mine, self.rz.at[self.z], self.dev(self.x, self.h * 4 + mate, self.k))
        self.c.send(mine, mine, self.rz.at[self.z], self.dev(self.x, self.f * 4 + self.z4, self.k))

    def z_mates(self):
        for mate in self.mates:
            landed(self.block(self.x, self.h, mate, self.k), self.rz.at[self.h * 4 + mate])
        self.x_send(None)
        self.c_send(self.x, self.h)

    def z_mirror(self):
        other = self.f * 4 + self.z4
        theirs = self.block(self.x, self.f, self.z4, self.k)
        landed(theirs, self.rz.at[other])
        for mate in self.mates:
            self.c.send(theirs, theirs, self.rz.at[other], self.dev(self.x, self.h * 4 + mate, self.k))
        self.x_send(self.z4)

    def z_far(self):
        for mate in self.mates:
            landed(self.block(self.x, self.f, mate, self.k), self.rz.at[self.f * 4 + mate])
            self.x_send(mate)
        self.c_send(self.x, self.f)

    def c_send(self, x, h):
        mine = self.half(x, h, self.k)
        self.c.send(mine, mine, self.rc, self.dev(self.x, self.z, 1 - self.k))

    def x_send(self, z4):
        mine, at = self.unit(self.x, z4)
        for way, x in enumerate(self.near_x):
            self.c.send(mine, mine, self.rn.at[at, way], self.dev(x, self.z, self.k))

    def x_near(self, z4):
        for way, x in enumerate(self.near_x):
            theirs, at = self.unit(x, z4)
            landed(theirs, self.rn.at[at, 1 - way])
        source, target = (self.x + 3 + 2 * self.k) % 4, (self.x + 1 + 2 * self.k) % 4
        passed, _ = self.unit(source, z4)
        self.c.send(passed, passed, self.rf.at[0 if z4 is None else 1], self.dev(target, self.z, self.k))

    def near_to_core(self, h):
        for x in self.near_x:
            self.c_send(x, h)

    def x_far(self, n):
        h = (self.h, self.f)[n]
        landed(self.half(self.far_x, h, self.k), self.rf.at[n])
        self.c_send(self.far_x, h)

    def c_wait(self):
        landed(self.buf.at[:, :, :, :, 1 - self.k], self.rc)

    def pair(self, *planes):
        return jnp.concatenate([self.buf[p].reshape(2048, 128) for p in planes], axis=1)


def band_weights(expanded, out, row_of, sign):
    lane = lax.broadcasted_iota(jnp.int32, (8, 2048), 1)
    sub = lax.broadcasted_iota(jnp.int32, (8, 2048), 0)
    tap = (sign * (lane - sub) + 1) & 7

    def one(t):
        rows = [expanded[pl.ds(row_of(t, j), 1), :] for j in range(3)]
        return jnp.where(tap == 0, rows[0], jnp.where(tap == 1, rows[1], jnp.where(tap == 2, rows[2], 0.0)))

    def body(u, carry):
        both = jnp.concatenate([one(2 * u), one(2 * u + 1)], axis=0)
        out[pl.ds(pl.multiple_of(16 * u, 16), 16), :] = both.astype(BF16)
        return carry

    lax.fori_loop(0, 18, body, 0)


def turned_weights(all_rows, spread, wide, k):
    row = lax.broadcasted_iota(jnp.int32, (64, 256), 0)
    col = lax.broadcasted_iota(jnp.int32, (64, 256), 1)
    source = jnp.where(row < 32, 2 * row + k, 2 * row - 63 - k)
    within = lax.broadcasted_iota(jnp.int32, (27, 128), 1) // 8 % 4
    for c in range(4):
        low, high = [all_rows[pl.ds(4 * q + c, 64, stride=8), :] for q in range(2)]
        mine = jnp.where(k == 0, low, high).T.astype(BF16)
        for n in range(8):
            pick = jnp.where(source == 8 * n + (col >> 5), 1.0, 0.0).astype(BF16)
            full = jnp.dot(mine, pick, preferred_element_type=F32)
            for half in range(2):
                spread[2 * n + half] = full[:, 128 * half : 128 * half + 128]
                total = spread[2 * n + half, pl.ds(0, 27, stride=4), :]
                for o in range(1, 4):
                    total = jnp.where(within == o, spread[2 * n + half, pl.ds(o, 27, stride=4), :], total)
                wide[32 * c : 32 * c + 27, 256 * n + 128 * half : 256 * n + 128 * half + 128] = total


def kernel(
    scale,
    x_hbm, w_hbm, bias_hbm, go_hbm,
    act_ref, ig_ref, out_ref,
    x_ref, w_ref, bias_ref, go_ref, load_sems,
    xb, gb, rep, wide, spread, wa, wb, dm, rows, t1, t2, t3, t4, all_rows, dw, yb, zb, tot, fo, fi, go_rim,
    send_sems, xz, xn, xf, xc, gz, gn, gf, gc, s1, s2, s3, sy, sz, sg, sf, so, ready,
):
    slab, chan = lax.axis_index("slab"), lax.axis_index("chan")
    y, zh = slab // NH, slab % NH
    x, z, k = chan // (NZ * NK), chan // NK % NZ, chan % NK
    place = (slab, x, z, k)
    copies = Copies(send_sems)
    gx_ = Gather(copies, place, xb, xz, xn, xf, xc)
    gg_ = Gather(copies, place, gb, gz, gn, gf, gc)
    h = gx_.h
    at = lambda yy, hh: (yy * NH + hh, chan)
    line = [(z + m) % NZ for m in range(1, NZ)]
    ring = [(x + m) % NX for m in range(1, NX)]
    after, before = ((slab + 1) % (NY * NH), chan), ((slab + NY * NH - 1) % (NY * NH), chan)

    def signal(sem, device):
        pl.semaphore_signal(sem, inc=1, device_id=device, device_id_type=MESH)

    partners = [gx_.dev(x, z, 1 - k)]
    partners += [gx_.dev(xx_, z, k) for xx_ in ring]
    partners += [gx_.dev(x, h * 4 + m, k) for m in gx_.mates] + [gx_.dev(x, gx_.f * 4 + gx_.z4, k)]
    partners += [at((y + m) % NY, zh) for m in range(1, NY)]
    barrier = pltpu.get_barrier_semaphore()
    for partner in partners:
        signal(barrier, partner)
    greets = {0: [at(y, 1), at(y, 3), at((y + NY - 1) % NY, 3)], 1: [at(y, 2)], 3: [at(y, 2)]}
    answers = {1: [at(y, 0)], 2: [at(y, 1), at(y, 3)], 3: [at(y, 0), at((y + 1) % NY, 0)]}
    for who, devices in greets.items():

        @pl.when(zh == who)
        def _(devices=devices):
            for device in devices:
                signal(barrier, device)

    loads = [
        pltpu.make_async_copy(source, target, load_sems.at[n])
        for n, (source, target) in enumerate(
            ((w_hbm, w_ref), (x_hbm, x_ref), (go_hbm, go_ref), (bias_hbm, bias_ref))
        )
    ]
    for load in loads:
        load.start()
    for n in range(8):
        row = lax.broadcasted_iota(jnp.int32, (256, 256), 0)
        col = lax.broadcasted_iota(jnp.int32, (256, 256), 1)
        rep[:, 256 * n : 256 * n + 256] = jnp.where(row == 32 * n + (col >> 3), 1.0, 0.0).astype(BF16)
    for load in loads:
        load.wait()
    for p in range(2):
        xb[p, x, h, gx_.z4, k] = x_ref[:, p].astype(F32).reshape(32, 128).astype(BF16)
    rows[104:128, :] = jnp.zeros((24, 256), F32)
    for t in range(27):
        rows[4 * t : 4 * t + 4, :] = w_ref[t].astype(F32)
    t1[...] = rows[...].T.reshape(4, 8, 8, 128).astype(BF16)
    by_tap = rows[...].astype(BF16)
    for n in range(8):
        wide[:, 256 * n : 256 * n + 256] = jnp.dot(
            by_tap, rep[:, 256 * n : 256 * n + 256], preferred_element_type=F32
        )
    band_weights(wide, wa, lambda t, j: t // 12 * 36 + j * 12 + t % 12, 1)

    pl.semaphore_wait(barrier, len(partners) + jnp.where(zh == 0, 0, jnp.where(zh == 1, 1, 2)))
    for who, devices in answers.items():

        @pl.when(zh == who)
        def _(devices=devices):
            for device in devices:
                signal(ready, device)

    gx_.z_send()
    gx_.z_mates()
    gx_.z_mirror()
    gx_.x_near(None)
    gx_.near_to_core(h)
    gx_.z_far()
    for zz in line:
        copies.send(t1.at[:, zz], t2.at[z], s1.at[z], gx_.dev(x, zz, k))
    t2[z] = t1[:, z]
    gx_.x_near(gx_.z4)
    gx_.x_far(0)
    for mate in gx_.mates:
        gx_.x_near(mate)
    gx_.near_to_core(gx_.f)
    gx_.x_far(1)

    for who, devices in greets.items():

        @pl.when(zh == who)
        def _(devices=devices):
            pl.semaphore_wait(ready, len(devices))

    copies.send(go_ref.at[:, 1], go_rim.at[0], so.at[0], after)
    copies.send(go_ref.at[:, 0], go_rim.at[1], so.at[1], before)
    gx_.c_wait()

    own = jnp.dot(wa[...], gx_.pair(0, 1), preferred_element_type=F32)

    def part(value, i, l, o, p):
        base = ((i * 3 + l) * 4 + o) * 8
        return value[base : base + 8, 128 * p : 128 * p + 128]

    def turned_sum(terms, sign):
        total = None
        for l in range(3):
            term = terms(l)
            term = term if l == 1 else pltpu.roll(term, sign * (1 - l) % 128, 1)
            total = term if total is None else total + term
        return total

    shares = [
        [turned_sum(lambda l: part(own, 2, l, o, 0), 1) for o in range(4)],
        [turned_sum(lambda l: part(own, 1, l, o, 0) + part(own, 2, l, o, 1), 1) for o in range(4)],
        [turned_sum(lambda l: part(own, 0, l, o, 0) + part(own, 1, l, o, 1), 1) for o in range(4)],
        [turned_sum(lambda l: part(own, 0, l, o, 1), 1) for o in range(4)],
    ]
    for o in range(4):
        for n in range(4):
            fo[n, o] = shares[n][o].astype(BF16)
    copies.send(fo.at[2:4], fi.at[0:2], sf.at[0], after)
    copies.send(fo.at[0:2], fi.at[2:4], sf.at[1], before)

    for zz in line:
        landed(t2.at[zz], s1.at[zz])
    for xx_ in ring:
        copies.send(t2.at[:, xx_], t3.at[x], s2.at[x], gx_.dev(xx_, z, k))
    t3[x] = t2[:, x]
    for xx_ in ring:
        landed(t3.at[xx_], s2.at[xx_])
    copies.send(t3, t4, s3, gx_.dev(x, z, 1 - k))
    landed(t4, s3)
    all_rows[0:256, :] = t3[...].astype(F32).reshape(256, 128)
    all_rows[256:512, :] = t4[...].astype(F32).reshape(256, 128)
    turned_weights(all_rows, spread, wide, k)
    band_weights(wide, wb, lambda t, j: t % 4 * 32 + t // 12 * 9 + j * 3 + t % 12 // 4, -1)

    landed(fi.at[0:2], sf.at[0])
    landed(fi.at[2:4], sf.at[1])
    for side in range(2):
        landed(go_rim.at[side], so.at[side])
    copies.drain()
    offsets = bias_ref[...].astype(F32)
    grads = []
    for n in range(4):
        row = []
        for o in range(4):
            pre = shares[n][o] + fi[n, o].astype(F32) + offsets[:, o : o + 1]
            sig = 1.0 / (1.0 + jnp.exp(-pre))
            if n in (1, 2):
                act_ref[o, n - 1] = (pre * sig).astype(BF16)
                given = go_ref[o, n - 1]
            else:
                given = go_rim[n // 3, o]
            row.append(given.astype(F32) * (sig * (1.0 + pre * (1.0 - sig))))
        grads.append(jnp.concatenate(row, axis=0).astype(BF16))
    for n in range(4):
        gb[n, x, h, gx_.z4, k] = grads[n]

    gg_.z_send()

    grads = [g.astype(F32) for g in grads]
    turns = [[g if l == 1 else pltpu.roll(g, (l - 1) % 128, 1) for l in range(3)] for g in grads]
    rolled = jnp.concatenate(
        [jnp.concatenate([turns[2 - i][l], turns[3 - i][l]], axis=1) for i in range(3) for l in range(3)], axis=0
    ).astype(BF16)
    lane = lax.broadcasted_iota(jnp.int32, (8, 2048), 1)
    sub = lax.broadcasted_iota(jnp.int32, (8, 2048), 0)
    tap = (lane - sub + 1) & 7
    whole = lax.dot_general(rolled, gx_.pair(0, 1), NT, preferred_element_type=F32)
    sums = []
    for i in range(3):
        full = whole[96 * i : 96 * i + 96].reshape(12, 8, 2048)
        for j in range(3):
            kept = jnp.where((tap == j)[None], full, 0.0)
            dm[96 * j : 96 * j + 96, :] = kept.reshape(96, 2048).astype(BF16)
        folded = lax.dot_general(dm[...], rep[...], NT, preferred_element_type=F32)
        sums.append(jnp.sum(folded.reshape(36, 8, 256), axis=1))
    per_o = jnp.sum((grads[1] + grads[2]).reshape(4, 8, 128), axis=(1, 2), keepdims=True).reshape(4, 1)
    sums.append(jnp.broadcast_to(per_o, (4, 256)))
    sums.append(jnp.zeros((16, 256), F32))
    dw[...] = jnp.concatenate(sums, axis=0).reshape(4, 32, 256).astype(BF16)
    for m in range(1, NY):
        copies.send(dw.at[(y + m) % NY], yb.at[y], sy.at[y], at((y + m) % NY, zh))

    yb[y] = dw[y]
    for m in range(1, NY):
        landed(yb.at[(y + m) % NY], sy.at[(y + m) % NY])
    zb[zh] = sum(yb[m].astype(F32) for m in range(NY)).astype(BF16)
    for s in (1, NH - 1):
        copies.send(zb.at[zh], zb.at[zh], sz.at[zh], at(y, (zh + s) % NH))

    gg_.z_mates()
    gg_.z_mirror()
    gg_.x_near(None)
    gg_.near_to_core(h)
    gg_.z_far()
    gg_.x_near(gg_.z4)
    for s in (1, NH - 1):
        landed(zb.at[(zh + s) % NH], sz.at[(zh + s) % NH])
    source, target = (zh + 3 + 2 * k) % NH, (zh + 1 + 2 * k) % NH
    copies.send(zb.at[source], zb.at[source], sz.at[source], at(y, target))
    gg_.x_far(0)
    for mate in gg_.mates:
        gg_.x_near(mate)
    gg_.near_to_core(gg_.f)
    gg_.x_far(1)
    gg_.c_wait()
    own2 = jnp.dot(wb[...], gg_.pair(1, 2), preferred_element_type=F32)
    outer = jnp.concatenate([wb[0:96, :], wb[192:288, :]], axis=0)
    rim = jnp.dot(outer, gg_.pair(0, 3), preferred_element_type=F32)
    for p in range(2):
        for c in range(4):
            if p == 0:
                terms = lambda l: part(own2, 0, l, c, 1) + part(own2, 1, l, c, 0) + part(rim, 1, l, c, 0)
            else:
                terms = lambda l: part(rim, 0, l, c, 1) + part(own2, 1, l, c, 1) + part(own2, 2, l, c, 0)
            ig_ref[c, p] = turned_sum(terms, -1).astype(BF16)
    landed(zb.at[(zh + 2) % NH], sz.at[(zh + 2) % NH])
    tot[y] = sum(zb[m].astype(F32) for m in range(NH)).astype(BF16)
    for m in range(1, NY):
        copies.send(tot.at[y], tot.at[y], sg.at[y], at((y + m) % NY, zh))
    for m in range(1, NY):
        landed(tot.at[(y + m) % NY], sg.at[(y + m) % NY])
    out_ref[...] = tot[...].astype(F32).reshape(128, 256) * scale
    copies.drain()


def finish(act_in, ig_in, sums, act_ref, ig_ref, wg_ref, bg_ref):
    act_ref[...] = act_in[...]
    ig_ref[...] = ig_in[...]
    for t in range(27):
        wg_ref[t] = sums[4 * t : 4 * t + 4, :]
    tail = sums[104:112, 0:128]
    lane = lax.broadcasted_iota(jnp.int32, (8, 128), 1)
    sub = lax.broadcasted_iota(jnp.int32, (8, 128), 0)
    bg_ref[...] = jnp.sum(jnp.where(sub == lane + 4, tail, 0.0), axis=0, keepdims=True)[:, 0:4]


def on_device(x_in, weight, bias_vec, grad_out):
    n_cells = lax.axis_size("slab") * x_in.shape[1] * x_in.shape[2] * x_in.shape[3]
    scale = 1.0 / math.sqrt(n_cells)
    dma = lambda *shape: pltpu.SemaphoreType.DMA(shape)
    vmem, anywhere = pl.BlockSpec(memory_space=pltpu.VMEM), pl.BlockSpec(memory_space=pl.ANY)
    held = lambda *args: pltpu.with_memory_space_constraint(*args, pltpu.VMEM)
    block = jax.ShapeDtypeStruct((4, 2, 8, 128), BF16)
    act, grad_in, sums = pl.pallas_call(
        functools.partial(kernel, scale),
        out_shape=(
            pltpu.VMEM((4, 2, 8, 128), BF16),
            pltpu.VMEM((4, 2, 8, 128), BF16),
            pltpu.VMEM((128, 256), F32),
        ),
        in_specs=[anywhere] * 4,
        out_specs=(vmem,) * 3,
        scratch_shapes=[
            pltpu.VMEM((4, 2, 8, 128), BF16),
            pltpu.VMEM((27, 4, 256), BF16),
            pltpu.VMEM((1, 4), BF16),
            pltpu.VMEM((4, 2, 8, 128), BF16),
            dma(4),
            pltpu.VMEM((2, NX, 2, 4, NK, 32, 128), BF16),
            pltpu.VMEM((4, NX, 2, 4, NK, 32, 128), BF16),
            pltpu.VMEM((256, 2048), BF16),
            pltpu.VMEM((128, 2048), F32),
            pltpu.VMEM((16, 128, 128), F32),
            pltpu.VMEM((288, 2048), BF16),
            pltpu.VMEM((288, 2048), BF16),
            pltpu.VMEM((288, 2048), BF16),
            pltpu.VMEM((128, 256), F32),
            pltpu.VMEM((NX, NZ, 8, 128), BF16),
            pltpu.VMEM((NZ, NX, 8, 128), BF16),
            pltpu.VMEM((NX, NZ, 8, 128), BF16),
            pltpu.VMEM((NX, NZ, 8, 128), BF16),
            pltpu.VMEM((512, 128), F32),
            pltpu.VMEM((4, 32, 256), BF16),
            pltpu.VMEM((4, 32, 256), BF16),
            pltpu.VMEM((4, 32, 256), BF16),
            pltpu.VMEM((4, 32, 256), BF16),
            pltpu.VMEM((4, 4, 8, 128), BF16),
            pltpu.VMEM((4, 4, 8, 128), BF16),
            pltpu.VMEM((2, 4, 8, 128), BF16),
            dma(48),
            dma(8), dma(5, 2), dma(2), pltpu.SemaphoreType.DMA,
            dma(8), dma(5, 2), dma(2), pltpu.SemaphoreType.DMA,
            dma(8), dma(4), pltpu.SemaphoreType.DMA,
            dma(4), dma(4), dma(4), dma(2), dma(2),
            pltpu.SemaphoreType.REGULAR,
        ],
        compiler_params=pltpu.CompilerParams(collective_id=0, has_side_effects=True),
    )(x_in, jnp.transpose(weight, (1, 0, 2)), bias_vec.reshape(1, 4), grad_out)
    act, grad_in, filters, bias_grad = pl.pallas_call(
        finish,
        out_shape=(
            block,
            block,
            jax.ShapeDtypeStruct((27, 4, 256), F32),
            jax.ShapeDtypeStruct((1, 4), F32),
        ),
        in_specs=[vmem] * 3,
        out_specs=(vmem,) * 4,
    )(held(act), held(grad_in), held(sums))
    return (act, grad_in, jnp.transpose(filters, (1, 0, 2)), bias_grad.reshape(4))


def solution(mesh):
    placed = (
        P("chan", "slab", None, None),
        P("chan", None, None),
        P("chan"),
        P("chan", "slab", None, None),
    )
    return jax.shard_map(
        on_device,
        mesh=mesh,
        in_specs=placed,
        out_specs=(
            P("chan", "slab", None, None),
            P("chan", "slab", None, None),
            P("chan", None, None),
            P("chan"),
        ),
        check_vma=False,
    )
```

```python
import functools
import math

import jax
import jax.numpy as jnp
from jax import lax
from jax.experimental import pallas as pl
from jax.experimental.pallas import tpu as pltpu
from jax.sharding import PartitionSpec as P

MESH = pl.DeviceIdType.MESH
F32, BF16 = jnp.float32, jnp.bfloat16
NX, NZ, NK = 4, 8, 2
NY, NH = 4, 4
NT = (((1,), (1,)), ((), ()))


class Copies:
    def __init__(self, send_sems):
        self.send_sems = send_sems
        self.started = []

    def send(self, src, dst, recv_sem, device):
        copy = pltpu.make_async_remote_copy(
            src_ref=src,
            dst_ref=dst,
            send_sem=self.send_sems.at[len(self.started)],
            recv_sem=recv_sem,
            device_id=device,
            device_id_type=MESH,
        )
        copy.start()
        self.started.append(copy)

    def drain(self):
        for copy in self.started:
            copy.wait_send()
        self.started = []


def landed(dst, recv_sem):
    here = (lax.axis_index("slab"), lax.axis_index("chan"))
    pltpu.make_async_remote_copy(
        src_ref=dst, dst_ref=dst, send_sem=recv_sem, recv_sem=recv_sem, device_id=here, device_id_type=MESH
    ).wait_recv()


class Gather:
    def __init__(self, copies, place, buf, rz, rn, rf, rc):
        self.c = copies
        self.slab, self.x, self.z, self.k = place
        self.h, self.z4 = self.z // 4, self.z % 4
        self.f = 1 - self.h
        self.mates = [(self.z4 + m) % 4 for m in range(1, 4)]
        self.near_x = [(self.x + step) % 4 for step in (1, 3)]
        self.far_x = (self.x + 2) % 4
        self.buf, self.rz, self.rn, self.rf, self.rc = buf, rz, rn, rf, rc

    def dev(self, x, z, k):
        return (self.slab, (x * NZ + z) * NK + k)

    def block(self, x, h, z4, k):
        return self.buf.at[:, x, h, z4, k]

    def half(self, x, h, k):
        return self.buf.at[:, x, h, :, k]

    def unit(self, x, z4):
        if z4 is None:
            return self.half(x, self.h, self.k), 4
        return self.block(x, self.f, z4, self.k), z4

    def z_send(self):
        mine = self.block(self.x, self.h, self.z4, self.k)
        for mate in self.mates:
            self.c.send(mine, mine, self.rz.at[self.z], self.dev(self.x, self.h * 4 + mate, self.k))
        self.c.send(mine, mine, self.rz.at[self.z], self.dev(self.x, self.f * 4 + self.z4, self.k))

    def z_mates(self):
        for mate in self.mates:
            landed(self.block(self.x, self.h, mate, self.k), self.rz.at[self.h * 4 + mate])
        self.x_send(None)
        self.c_send(self.x, self.h)

    def z_mirror(self):
        other = self.f * 4 + self.z4
        theirs = self.block(self.x, self.f, self.z4, self.k)
        landed(theirs, self.rz.at[other])
        for mate in self.mates:
            self.c.send(theirs, theirs, self.rz.at[other], self.dev(self.x, self.h * 4 + mate, self.k))
        self.x_send(self.z4)

    def z_far(self):
        for mate in self.mates:
            landed(self.block(self.x, self.f, mate, self.k), self.rz.at[self.f * 4 + mate])
            self.x_send(mate)
        self.c_send(self.x, self.f)

    def c_send(self, x, h):
        mine = self.half(x, h, self.k)
        self.c.send(mine, mine, self.rc, self.dev(self.x, self.z, 1 - self.k))

    def x_send(self, z4):
        mine, at = self.unit(self.x, z4)
        for way, x in enumerate(self.near_x):
            self.c.send(mine, mine, self.rn.at[at, way], self.dev(x, self.z, self.k))

    def x_near(self, z4):
        for way, x in enumerate(self.near_x):
            theirs, at = self.unit(x, z4)
            landed(theirs, self.rn.at[at, 1 - way])
        source, target = (self.x + 3 + 2 * self.k) % 4, (self.x + 1 + 2 * self.k) % 4
        passed, _ = self.unit(source, z4)
        self.c.send(passed, passed, self.rf.at[0 if z4 is None else 1], self.dev(target, self.z, self.k))

    def near_to_core(self, h):
        for x in self.near_x:
            self.c_send(x, h)

    def x_far(self, n):
        h = (self.h, self.f)[n]
        landed(self.half(self.far_x, h, self.k), self.rf.at[n])
        self.c_send(self.far_x, h)

    def c_wait(self):
        landed(self.buf.at[:, :, :, :, 1 - self.k], self.rc)

    def pair(self, *planes):
        return jnp.concatenate([self.buf[p].reshape(2048, 128) for p in planes], axis=1)


def band_weights(expanded, out, row_of, sign):
    lane = lax.broadcasted_iota(jnp.int32, (8, 2048), 1)
    sub = lax.broadcasted_iota(jnp.int32, (8, 2048), 0)
    tap = (sign * (lane - sub) + 1) & 7

    def one(t):
        rows = [expanded[pl.ds(row_of(t, j), 1), :] for j in range(3)]
        return jnp.where(tap == 0, rows[0], jnp.where(tap == 1, rows[1], jnp.where(tap == 2, rows[2], 0.0)))

    def body(u, carry):
        both = jnp.concatenate([one(2 * u), one(2 * u + 1)], axis=0)
        out[pl.ds(pl.multiple_of(16 * u, 16), 16), :] = both.astype(BF16)
        return carry

    lax.fori_loop(0, 18, body, 0)


def turned_weights(all_rows, spread, wide, k):
    row = lax.broadcasted_iota(jnp.int32, (64, 256), 0)
    col = lax.broadcasted_iota(jnp.int32, (64, 256), 1)
    source = jnp.where(row < 32, 2 * row + k, 2 * row - 63 - k)
    within = lax.broadcasted_iota(jnp.int32, (27, 128), 1) // 8 % 4
    for c in range(4):
        low, high = [all_rows[pl.ds(4 * q + c, 64, stride=8), :] for q in range(2)]
        mine = jnp.where(k == 0, low, high).T.astype(BF16)
        for n in range(8):
            pick = jnp.where(source == 8 * n + (col >> 5), 1.0, 0.0).astype(BF16)
            full = jnp.dot(mine, pick, preferred_element_type=F32)
            for half in range(2):
                spread[2 * n + half] = full[:, 128 * half : 128 * half + 128]
                total = spread[2 * n + half, pl.ds(0, 27, stride=4), :]
                for o in range(1, 4):
                    total = jnp.where(within == o, spread[2 * n + half, pl.ds(o, 27, stride=4), :], total)
                wide[32 * c : 32 * c + 27, 256 * n + 128 * half : 256 * n + 128 * half + 128] = total


def kernel(
    scale,
    x_hbm, w_hbm, bias_hbm, go_hbm,
    act_ref, ig_ref, out_ref,
    x_ref, w_ref, bias_ref, go_ref, load_sems,
    xb, gb, rep, wide, spread, wa, wb, dm, rows, t1, t2, t3, t4, all_rows, dw, yb, zb, tot, fo, fi, go_rim,
    send_sems, xz, xn, xf, xc, gz, gn, gf, gc, s1, s2, s3, sy, sz, sg, sf, so, pass_sem, ready,
):
    slab, chan = lax.axis_index("slab"), lax.axis_index("chan")
    y, zh = slab // NH, slab % NH
    x, z, k = chan // (NZ * NK), chan // NK % NZ, chan % NK
    place = (slab, x, z, k)
    copies = Copies(send_sems)
    gx_ = Gather(copies, place, xb, xz, xn, xf, xc)
    gg_ = Gather(copies, place, gb, gz, gn, gf, gc)
    h = gx_.h
    at = lambda yy, hh: (yy * NH + hh, chan)
    line = [(z + m) % NZ for m in range(1, NZ)]
    ring = [(x + m) % NX for m in range(1, NX)]
    after, before = ((slab + 1) % (NY * NH), chan), ((slab + NY * NH - 1) % (NY * NH), chan)

    def signal(sem, device):
        pl.semaphore_signal(sem, inc=1, device_id=device, device_id_type=MESH)

    partners = [gx_.dev(x, z, 1 - k)]
    partners += [gx_.dev(xx_, z, k) for xx_ in ring]
    partners += [gx_.dev(x, h * 4 + m, k) for m in gx_.mates] + [gx_.dev(x, gx_.f * 4 + gx_.z4, k)]
    partners += [at((y + m) % NY, zh) for m in range(1, NY)]
    barrier = pltpu.get_barrier_semaphore()
    for partner in partners:
        signal(barrier, partner)
    greets = {0: [at(y, 1), at(y, 3), at((y + NY - 1) % NY, 3)], 1: [at(y, 2)], 3: [at(y, 2)]}
    answers = {1: [at(y, 0)], 2: [at(y, 1), at(y, 3)], 3: [at(y, 0), at((y + 1) % NY, 0)]}
    for who, devices in greets.items():

        @pl.when(zh == who)
        def _(devices=devices):
            for device in devices:
                signal(barrier, device)

    loads = [
        pltpu.make_async_copy(source, target, load_sems.at[n])
        for n, (source, target) in enumerate(
            ((w_hbm, w_ref), (x_hbm, x_ref), (go_hbm, go_ref), (bias_hbm, bias_ref))
        )
    ]
    for load in loads:
        load.start()
    for n in range(8):
        row = lax.broadcasted_iota(jnp.int32, (256, 256), 0)
        col = lax.broadcasted_iota(jnp.int32, (256, 256), 1)
        rep[:, 256 * n : 256 * n + 256] = jnp.where(row == 32 * n + (col >> 3), 1.0, 0.0).astype(BF16)
    for load in loads:
        load.wait()
    for p in range(2):
        xb[p, x, h, gx_.z4, k] = x_ref[:, p].astype(F32).reshape(32, 128).astype(BF16)
    rows[104:128, :] = jnp.zeros((24, 256), F32)
    for t in range(27):
        rows[4 * t : 4 * t + 4, :] = w_ref[t].astype(F32)
    t1[...] = rows[...].T.reshape(4, 8, 8, 128).astype(BF16)
    by_tap = rows[...].astype(BF16)
    for n in range(8):
        wide[:, 256 * n : 256 * n + 256] = jnp.dot(
            by_tap, rep[:, 256 * n : 256 * n + 256], preferred_element_type=F32
        )
    band_weights(wide, wa, lambda t, j: t // 12 * 36 + j * 12 + t % 12, 1)

    pl.semaphore_wait(barrier, len(partners) + jnp.where(zh == 0, 0, jnp.where(zh == 1, 1, 2)))
    for who, devices in answers.items():

        @pl.when(zh == who)
        def _(devices=devices):
            for device in devices:
                signal(ready, device)

    gx_.z_send()
    gx_.z_mates()
    gx_.z_mirror()
    gx_.x_near(None)
    gx_.near_to_core(h)
    gx_.z_far()
    for zz in line:
        copies.send(t1.at[:, zz], t2.at[z], s1.at[z], gx_.dev(x, zz, k))
    t2[z] = t1[:, z]
    gx_.x_near(gx_.z4)
    gx_.x_far(0)
    for mate in gx_.mates:
        gx_.x_near(mate)
    gx_.near_to_core(gx_.f)
    gx_.x_far(1)

    for who, devices in greets.items():

        @pl.when(zh == who)
        def _(devices=devices):
            pl.semaphore_wait(ready, len(devices))

    copies.send(go_ref.at[:, 1], go_rim.at[0], so.at[0], after)
    copies.send(go_ref.at[:, 0], go_rim.at[1], so.at[1], before)
    gx_.c_wait()

    own = jnp.dot(wa[...], gx_.pair(0, 1), preferred_element_type=F32)

    def part(value, i, l, o, p):
        base = ((i * 3 + l) * 4 + o) * 8
        return value[base : base + 8, 128 * p : 128 * p + 128]

    def turned_sum(terms, sign):
        total = None
        for l in range(3):
            term = terms(l)
            term = term if l == 1 else pltpu.roll(term, sign * (1 - l) % 128, 1)
            total = term if total is None else total + term
        return total

    shares = [
        [turned_sum(lambda l: part(own, 2, l, o, 0), 1) for o in range(4)],
        [turned_sum(lambda l: part(own, 1, l, o, 0) + part(own, 2, l, o, 1), 1) for o in range(4)],
        [turned_sum(lambda l: part(own, 0, l, o, 0) + part(own, 1, l, o, 1), 1) for o in range(4)],
        [turned_sum(lambda l: part(own, 0, l, o, 1), 1) for o in range(4)],
    ]
    for o in range(4):
        for n in range(4):
            fo[n, o] = shares[n][o].astype(BF16)
    copies.send(fo.at[2:4], fi.at[0:2], sf.at[0], after)
    copies.send(fo.at[0:2], fi.at[2:4], sf.at[1], before)

    for zz in line:
        landed(t2.at[zz], s1.at[zz])
    for xx_ in ring:
        copies.send(t2.at[:, xx_], t3.at[x], s2.at[x], gx_.dev(xx_, z, k))
    t3[x] = t2[:, x]
    for xx_ in ring:
        landed(t3.at[xx_], s2.at[xx_])
    copies.send(t3, t4, s3, gx_.dev(x, z, 1 - k))
    landed(t4, s3)
    landed(fi.at[0:2], sf.at[0])
    landed(fi.at[2:4], sf.at[1])
    for side in range(2):
        landed(go_rim.at[side], so.at[side])
    copies.drain()
    offsets = bias_ref[...].astype(F32)
    grads = []
    for n in range(4):
        row = []
        for o in range(4):
            pre = shares[n][o] + fi[n, o].astype(F32) + offsets[:, o : o + 1]
            sig = 1.0 / (1.0 + jnp.exp(-pre))
            if n in (1, 2):
                act_ref[o, n - 1] = (pre * sig).astype(BF16)
                given = go_ref[o, n - 1]
            else:
                given = go_rim[n // 3, o]
            row.append(given.astype(F32) * (sig * (1.0 + pre * (1.0 - sig))))
        grads.append(jnp.concatenate(row, axis=0).astype(BF16))
    for n in range(4):
        gb[n, x, h, gx_.z4, k] = grads[n]

    gg_.z_send()

    grads = [g.astype(F32) for g in grads]
    turns = [[g if l == 1 else pltpu.roll(g, (l - 1) % 128, 1) for l in range(3)] for g in grads]
    rolled = jnp.concatenate(
        [jnp.concatenate([turns[2 - i][l], turns[3 - i][l]], axis=1) for i in range(3) for l in range(3)], axis=0
    ).astype(BF16)
    lane = lax.broadcasted_iota(jnp.int32, (8, 2048), 1)
    sub = lax.broadcasted_iota(jnp.int32, (8, 2048), 0)
    tap = (lane - sub + 1) & 7
    whole = lax.dot_general(rolled, gx_.pair(0, 1), NT, preferred_element_type=F32)
    sums = []
    for i in range(3):
        full = whole[96 * i : 96 * i + 96].reshape(12, 8, 2048)
        for j in range(3):
            kept = jnp.where((tap == j)[None], full, 0.0)
            dm[96 * j : 96 * j + 96, :] = kept.reshape(96, 2048).astype(BF16)
        folded = lax.dot_general(dm[...], rep[...], NT, preferred_element_type=F32)
        sums.append(jnp.sum(folded.reshape(36, 8, 256), axis=1))
    per_o = jnp.sum((grads[1] + grads[2]).reshape(4, 8, 128), axis=(1, 2), keepdims=True).reshape(4, 1)
    sums.append(jnp.broadcast_to(per_o, (4, 256)))
    sums.append(jnp.zeros((16, 256), F32))
    dw[...] = jnp.concatenate(sums, axis=0).reshape(4, 32, 256).astype(BF16)
    for m in range(1, NY):
        copies.send(dw.at[(y + m) % NY], yb.at[y], sy.at[y], at((y + m) % NY, zh))

    all_rows[0:256, :] = t3[...].astype(F32).reshape(256, 128)
    all_rows[256:512, :] = t4[...].astype(F32).reshape(256, 128)
    turned_weights(all_rows, spread, wide, k)
    band_weights(wide, wb, lambda t, j: t % 4 * 32 + t // 12 * 9 + j * 3 + t % 12 // 4, -1)

    yb[y] = dw[y]
    for m in range(1, NY):
        landed(yb.at[(y + m) % NY], sy.at[(y + m) % NY])
    zb[zh] = sum(yb[m].astype(F32) for m in range(NY)).astype(BF16)
    for s in (1, NH - 1):
        copies.send(zb.at[zh], zb.at[zh], sz.at[zh], at(y, (zh + s) % NH))

    source, target = (zh + 3 + 2 * k) % NH, (zh + 1 + 2 * k) % NH
    passed = pltpu.make_async_remote_copy(
        src_ref=zb.at[source],
        dst_ref=zb.at[source],
        send_sem=pass_sem,
        recv_sem=sz.at[source],
        device_id=at(y, target),
        device_id_type=MESH,
    )

    def pass_on():
        landed(zb.at[source], sz.at[source])
        passed.start()

    gg_.z_mates()
    gg_.z_mirror()
    gg_.x_near(None)
    gg_.near_to_core(h)

    @pl.when(zh % 2 == 1)
    def _():
        pass_on()

    gg_.z_far()
    gg_.x_near(gg_.z4)
    @pl.when(zh % 2 == 0)
    def _():
        pass_on()

    gg_.x_far(0)
    for mate in gg_.mates:
        gg_.x_near(mate)
    gg_.near_to_core(gg_.f)
    for m in (target, (zh + 2) % NH):
        landed(zb.at[m], sz.at[m])
    tot[y] = sum(zb[m].astype(F32) for m in range(NH)).astype(BF16)
    for m in range(1, NY):
        copies.send(tot.at[y], tot.at[y], sg.at[y], at((y + m) % NY, zh))
    gg_.x_far(1)
    gg_.c_wait()
    own2 = jnp.dot(wb[...], gg_.pair(1, 2), preferred_element_type=F32)
    outer = jnp.concatenate([wb[0:96, :], wb[192:288, :]], axis=0)
    rim = jnp.dot(outer, gg_.pair(0, 3), preferred_element_type=F32)
    for p in range(2):
        for c in range(4):
            if p == 0:
                terms = lambda l: part(own2, 0, l, c, 1) + part(own2, 1, l, c, 0) + part(rim, 1, l, c, 0)
            else:
                terms = lambda l: part(rim, 0, l, c, 1) + part(own2, 1, l, c, 1) + part(own2, 2, l, c, 0)
            ig_ref[c, p] = turned_sum(terms, -1).astype(BF16)
    for m in range(1, NY):
        landed(tot.at[(y + m) % NY], sg.at[(y + m) % NY])
    out_ref[...] = tot[...].astype(F32).reshape(128, 256) * scale
    passed.wait_send()
    copies.drain()


def finish(act_in, ig_in, sums, act_ref, ig_ref, wg_ref, bg_ref):
    act_ref[...] = act_in[...]
    ig_ref[...] = ig_in[...]
    for t in range(27):
        wg_ref[t] = sums[4 * t : 4 * t + 4, :]
    tail = sums[104:112, 0:128]
    lane = lax.broadcasted_iota(jnp.int32, (8, 128), 1)
    sub = lax.broadcasted_iota(jnp.int32, (8, 128), 0)
    bg_ref[...] = jnp.sum(jnp.where(sub == lane + 4, tail, 0.0), axis=0, keepdims=True)[:, 0:4]


def on_device(x_in, weight, bias_vec, grad_out):
    n_cells = lax.axis_size("slab") * x_in.shape[1] * x_in.shape[2] * x_in.shape[3]
    scale = 1.0 / math.sqrt(n_cells)
    dma = lambda *shape: pltpu.SemaphoreType.DMA(shape)
    vmem, anywhere = pl.BlockSpec(memory_space=pltpu.VMEM), pl.BlockSpec(memory_space=pl.ANY)
    held = lambda *args: pltpu.with_memory_space_constraint(*args, pltpu.VMEM)
    block = jax.ShapeDtypeStruct((4, 2, 8, 128), BF16)
    act, grad_in, sums = pl.pallas_call(
        functools.partial(kernel, scale),
        out_shape=(
            pltpu.VMEM((4, 2, 8, 128), BF16),
            pltpu.VMEM((4, 2, 8, 128), BF16),
            pltpu.VMEM((128, 256), F32),
        ),
        in_specs=[anywhere] * 4,
        out_specs=(vmem,) * 3,
        scratch_shapes=[
            pltpu.VMEM((4, 2, 8, 128), BF16),
            pltpu.VMEM((27, 4, 256), BF16),
            pltpu.VMEM((1, 4), BF16),
            pltpu.VMEM((4, 2, 8, 128), BF16),
            dma(4),
            pltpu.VMEM((2, NX, 2, 4, NK, 32, 128), BF16),
            pltpu.VMEM((4, NX, 2, 4, NK, 32, 128), BF16),
            pltpu.VMEM((256, 2048), BF16),
            pltpu.VMEM((128, 2048), F32),
            pltpu.VMEM((16, 128, 128), F32),
            pltpu.VMEM((288, 2048), BF16),
            pltpu.VMEM((288, 2048), BF16),
            pltpu.VMEM((288, 2048), BF16),
            pltpu.VMEM((128, 256), F32),
            pltpu.VMEM((NX, NZ, 8, 128), BF16),
            pltpu.VMEM((NZ, NX, 8, 128), BF16),
            pltpu.VMEM((NX, NZ, 8, 128), BF16),
            pltpu.VMEM((NX, NZ, 8, 128), BF16),
            pltpu.VMEM((512, 128), F32),
            pltpu.VMEM((4, 32, 256), BF16),
            pltpu.VMEM((4, 32, 256), BF16),
            pltpu.VMEM((4, 32, 256), BF16),
            pltpu.VMEM((4, 32, 256), BF16),
            pltpu.VMEM((4, 4, 8, 128), BF16),
            pltpu.VMEM((4, 4, 8, 128), BF16),
            pltpu.VMEM((2, 4, 8, 128), BF16),
            dma(48),
            dma(8), dma(5, 2), dma(2), pltpu.SemaphoreType.DMA,
            dma(8), dma(5, 2), dma(2), pltpu.SemaphoreType.DMA,
            dma(8), dma(4), pltpu.SemaphoreType.DMA,
            dma(4), dma(4), dma(4), dma(2), dma(2), pltpu.SemaphoreType.DMA,
            pltpu.SemaphoreType.REGULAR,
        ],
        compiler_params=pltpu.CompilerParams(collective_id=0, has_side_effects=True),
    )(x_in, jnp.transpose(weight, (1, 0, 2)), bias_vec.reshape(1, 4), grad_out)
    act, grad_in, filters, bias_grad = pl.pallas_call(
        finish,
        out_shape=(
            block,
            block,
            jax.ShapeDtypeStruct((27, 4, 256), F32),
            jax.ShapeDtypeStruct((1, 4), F32),
        ),
        in_specs=[vmem] * 3,
        out_specs=(vmem,) * 4,
    )(held(act), held(grad_in), held(sums))
    return (act, grad_in, jnp.transpose(filters, (1, 0, 2)), bias_grad.reshape(4))


def solution(mesh):
    placed = (
        P("chan", "slab", None, None),
        P("chan", None, None),
        P("chan"),
        P("chan", "slab", None, None),
    )
    return jax.shard_map(
        on_device,
        mesh=mesh,
        in_specs=placed,
        out_specs=(
            P("chan", "slab", None, None),
            P("chan", "slab", None, None),
            P("chan", None, None),
            P("chan"),
        ),
        check_vma=False,
    )
```
